32 devices in a mesh: district: 16 (over z, y, x), coarse: 2 (over core).
Axes of the slice: x: 2, y: 2, z: 4, core: 2. Of those that a mesh axis runs over, the one named last changes fastest.
Arguments:
- free_response: float32 [128, 16, 512], P(('district', 'coarse')), may hold values from -6 to 6
- flexibility: bfloat16 [128, 512, 512], P(('district', 'coarse')), as said below
- corner_modes: bfloat16 [128, 8, 512], P(('district', 'coarse')), may hold values from -0.5 to 0.5
- corner_owner: int32 [128, 8], P(('district', 'coarse')), may hold values from 0 to 255
- coarse_inverse: float32 [16, 256, 256], P('district'), as said below
- iface_blocks: int32 [128], P(('district', 'coarse')), may hold values from 2 to 4, as said below
- partner: int32 [128, 4], P(('district', 'coarse')), may hold values from -1 to 511, as said below
Outputs:
- multiplier: float32 [128, 16, 512], P(('district', 'coarse'))
- residual: float32 [128, 16, 512], P(('district', 'coarse'))
The draws below stay inside these ranges and needn't reach their ends.
Inputs may be any that keep to these rules, and one draw needn't show every extreme that they name: `iface_blocks`: every subdomain uses 128 times this many interface unknowns, its first blocks. partner[s, b] is the global block index of the block that shares interface block b of subdomain s; pairs are mutual. Unused blocks, and used blocks against the ground, hold -1. A partner lies on the same coarse index and on the next or previous district index (district closes into a loop). Exactly 4 blocks of each device pair with blocks of the next device along district, and so exactly 4 with the previous one; no block pairs within its own device. `flexibility`: symmetric positive definite, every eigenvalue between 1/2 and 10. `coarse_inverse`: symmetric positive definite, every eigenvalue between 1/2 and 10.
All inputs are finite; a program needn't handle non-finite values.
Results may differ from the reference program's by a relative error of at most 0.007.
Values sent between devices are 32-bit elements; how exact they have to be, the bound alone decides.
No kernel may reach another device: no remote copies, remote signals or barrier semaphores. Data moves between devices by JAX's collectives and lax.ppermute only.
A program may use at most 64 MiB of HBM per device.

```python
import jax
import jax.numpy as jnp
from jax import lax

M = 512
BLK = 128
NBLK = 4
R = 16
KC = 8
NCD = 256
SLOTS = 4
ITERS = 2
SIDE = 4
SUBS = 128
N_DISTRICT = 16
N_COARSE = 2


def layout_draw(key):
    base_key = jax.random.fold_in(key, 11)
    key_live, key_score = jax.random.split(base_key)
    dist_count = N_DISTRICT
    coarse_count = N_COARSE
    per_device = SLOTS * NBLK
    live_count = jax.random.randint(key_live, (dist_count, coarse_count, SLOTS), 2, NBLK + 1)
    position = jnp.arange(per_device)
    slot_of = position // NBLK
    block_of = position % NBLK
    used_block = block_of[None, None, :] < live_count[:, :, slot_of]
    scores = jax.random.randint(key_score, (dist_count, coarse_count, per_device), 0, 4096) * per_device + position[None, None, :]
    scores = jnp.where(used_block, scores, -1 - position[None, None, :])
    ranked = jnp.argsort(-scores, axis=-1)
    right_pos = ranked[:, :, :SIDE]
    left_pos = ranked[:, :, SIDE:2 * SIDE]
    device_base = (jnp.arange(dist_count)[:, None] * coarse_count + jnp.arange(coarse_count)[None, :]) * per_device
    right_gid = device_base[:, :, None] + right_pos
    left_gid = device_base[:, :, None] + left_pos
    to_right = jnp.roll(left_gid, -1, axis=0)
    to_left = jnp.roll(right_gid, 1, axis=0)
    right_hit = position[None, None, :, None] == right_pos[:, :, None, :]
    left_hit = position[None, None, :, None] == left_pos[:, :, None, :]
    partner = -1 + jnp.sum(jnp.where(right_hit, to_right[:, :, None, :] + 1, 0), axis=-1) + jnp.sum(jnp.where(left_hit, to_left[:, :, None, :] + 1, 0), axis=-1)
    return (live_count.reshape(-1).astype(jnp.int32), partner.reshape(dist_count * coarse_count * SLOTS, NBLK).astype(jnp.int32))


def draw_iface_blocks(key, part):
    return layout_draw(key)[0]


def draw_partner(key, part):
    return layout_draw(key)[1]


def definite_draw(key, item_count, mat_order, out_dtype):
    key_list = jax.random.split(key, item_count)
    spread_scale = 3.0

    def draw_single(item_key):
        key_fac, key_diag = jax.random.split(item_key)
        factor = jax.random.uniform(key_fac, (mat_order, mat_order), jnp.float32, -1.0, 1.0)
        gram_part = jnp.dot(factor, factor.T, precision=lax.Precision.HIGHEST) * (spread_scale / mat_order)
        gram_part = 0.5 * (gram_part + gram_part.T)
        diag_part = jax.random.uniform(key_diag, (mat_order,), jnp.float32, 1.0, 2.0)
        return (gram_part + jnp.diag(diag_part)).astype(out_dtype)
    return lax.map(draw_single, key_list)


def draw_flexibility(key, part):
    return definite_draw(jax.random.fold_in(key, 3), SUBS, M, jnp.bfloat16)


def draw_coarse_inverse(key, part):
    return definite_draw(jax.random.fold_in(key, 5), N_DISTRICT, NCD, jnp.float32)


def touch_ends(values, key, smallest, largest):
    place = [jax.random.randint(jax.random.fold_in(key, axis), (), 0, length) for axis, length in enumerate(values.shape)]
    widest = values.shape.index(max(values.shape))
    next_to = place[:widest] + [(place[widest] + 1) % values.shape[widest]] + place[widest + 1:]
    return values.at[tuple(place)].set(smallest).at[tuple(next_to)].set(largest)


def block_scale(rng, shape, cuts, least, largest):
    loudness, own = 1.0, jax.random.fold_in(rng, 6)
    for dim, shards_of in cuts:
        steps = jnp.exp(jax.random.uniform(jax.random.fold_in(own, dim), (shards_of,), jnp.float32, least / len(cuts), largest / len(cuts)))
        loudness = loudness * jnp.repeat(steps, shape[dim] // shards_of).reshape([-1 if axis == dim else 1 for axis in range(len(shape))])
    return loudness


def normal_values(key, extent, scale, reach, cuts=(), held_as=jnp.bfloat16):
    result = scale * jax.random.normal(key, extent, jnp.float32)
    if cuts:
        result = result * block_scale(key, extent, cuts, -0.22, 0.18)
    return jnp.clip(result, -reach, reach).astype(held_as)


def setup_inputs(seed: int = 0) -> dict:
    keys = jax.random.split(jax.random.key(seed), 8)
    return {
        "free_response": normal_values(keys[0], (SUBS, R, M), 1.0, 6.0, ((0, 32),), jnp.float32),
        "flexibility": draw_flexibility(jax.random.fold_in(keys[7], 71), 0),
        "corner_modes": normal_values(keys[2], (SUBS, KC, M), (M // 4) ** -0.5, 0.5, ((0, 32),)),
        "corner_owner": touch_ends(jax.random.randint(keys[3], (SUBS, KC), 0, NCD), jax.random.fold_in(keys[3], 1), 0, NCD - 1).astype(jnp.int32),
        "coarse_inverse": draw_coarse_inverse(jax.random.fold_in(keys[7], 71), 0),
        "iface_blocks": draw_iface_blocks(jax.random.fold_in(keys[7], 71), 0),
        "partner": draw_partner(jax.random.fold_in(keys[7], 71), 0),
    }


def reference(free_response, flexibility, corner_modes, corner_owner, coarse_inverse, iface_blocks, partner):
    sub_count = free_response.shape[0]
    group_count = N_DISTRICT
    per_group = sub_count // group_count
    used_block = (jnp.arange(NBLK)[None, :] < iface_blocks[:, None]).reshape(-1)
    flat_partner = partner.reshape(-1)
    paired = flat_partner >= 0
    safe_partner = jnp.maximum(flat_partner, 0)

    def jump_of(response):
        u_blocks = response.reshape(sub_count, R, NBLK, BLK).transpose(0, 2, 1, 3).reshape(sub_count * NBLK, R, BLK)
        across = jnp.where(paired[:, None, None], u_blocks[safe_partner], jnp.float32(0.0))
        jumped = jnp.where(used_block[:, None, None], u_blocks - across, jnp.float32(0.0))
        return jumped.reshape(sub_count, NBLK, R, BLK).transpose(0, 2, 1, 3).reshape(sub_count, R, M)

    mode_rows = corner_modes.astype(jnp.float32)
    one_hot = (corner_owner[:, :, None] == jnp.arange(NCD)[None, None, :]).astype(jnp.float32)
    owner_index = jnp.broadcast_to(corner_owner[:, None, :], (sub_count, R, KC)).astype(jnp.int32)

    def local_part(operands):
        block_forces, matrices = operands
        return jnp.einsum("srm,smn->srn", block_forces.astype(jnp.float32), matrices.astype(jnp.float32), precision=lax.Precision.HIGHEST)

    def apply_operator(field):
        forces = field.astype(jnp.bfloat16)
        local_term = lax.map(local_part, (forces.reshape(group_count, per_group, R, M), flexibility.reshape(group_count, per_group, M, M)))
        local_term = local_term.reshape(sub_count, R, M)
        corner_sums = jnp.einsum("srm,skm->srk", forces.astype(jnp.float32), mode_rows, precision=lax.Precision.HIGHEST)
        contrib = jnp.einsum("srk,skc->src", corner_sums, one_hot, precision=lax.Precision.HIGHEST)
        coarse_res = contrib.reshape(group_count, per_group, R, NCD).sum(axis=1)
        coarse_sol = jnp.einsum("grc,gcd->grd", coarse_res, coarse_inverse, precision=lax.Precision.HIGHEST)
        z_sub = jnp.repeat(coarse_sol, per_group, axis=0)
        corner_values = jnp.take_along_axis(z_sub, owner_index, axis=2).astype(jnp.bfloat16)
        response = local_term + jnp.einsum("srk,skm->srm", corner_values.astype(jnp.float32), mode_rows, precision=lax.Precision.HIGHEST)
        return jump_of(response)

    rhs = jump_of(free_response)
    multiplier = jnp.zeros_like(rhs)
    residual = rhs
    direction = rhs
    norm_now = jnp.sum(residual * residual)
    for turn_index in range(ITERS):
        image = apply_operator(direction)
        step_size = norm_now / jnp.sum(direction * image)
        multiplier = multiplier + step_size * direction
        residual = residual - step_size * image
        if turn_index + 1 < ITERS:
            norm_next = jnp.sum(residual * residual)
            direction = residual + (norm_next / norm_now) * direction
            norm_now = norm_next
    return multiplier, residual
```

```python
import functools

import jax
import jax.numpy as jnp
from jax import lax
from jax.experimental import pallas as pl
from jax.experimental.pallas import tpu as pltpu
from jax.sharding import PartitionSpec as P

ITERS = 2
SIDE = 4
AXES = ("district", "coarse")
VMEM = pl.BlockSpec(memory_space=pltpu.VMEM)
SMEM = pl.BlockSpec(memory_space=pltpu.SMEM)
F32 = jnp.float32
BF16 = jnp.bfloat16
TILE = 8
LANES = 128


def quotient(value, by):
    if by & (by - 1) == 0:
        return lax.shift_right_logical(value, jnp.int32(by.bit_length() - 1))
    return lax.div(value, jnp.int32(by))


def remainder(value, by):
    if by & (by - 1) == 0:
        return lax.bitwise_and(value, jnp.int32(by - 1))
    return lax.rem(value, jnp.int32(by))


def near_side(index):
    return jnp.where(remainder(index, 2) == 0, index + 1, index - 1)


def far_side(index, count):
    return jnp.where(
        remainder(index, 2) == 0,
        jnp.where(index == 0, count - 1, index - 1),
        jnp.where(index == count - 1, 0, index + 1),
    )


def facing(partner_ref, dims):
    index = lax.axis_index("district")
    near = near_side(index)
    far = far_side(index, dims.districts)
    out = []
    for slot in range(dims.slots):
        for block in range(dims.blocks):
            place = partner_ref[slot, block]
            paired = place >= 0
            safe = jnp.maximum(place, 0)
            district = quotient(safe, dims.coarse * dims.per_device)
            out.append(
                (
                    jnp.logical_and(paired, district == near).astype(jnp.int32),
                    jnp.logical_and(paired, district == far).astype(jnp.int32),
                    remainder(safe, dims.per_device),
                )
            )
    return out


def block_of(dims, ref, slot, block):
    return ref[slot, :, block * LANES : (block + 1) * LANES]


def pack_first_kernel(dims, partner_ref, free_ref, near_ref, far_ref, order):
    near_count = jnp.int32(0)
    far_count = jnp.int32(0)
    for place, (near, far, _) in enumerate(facing(partner_ref, dims)):
        slot = jnp.where(near > 0, near_count, jnp.where(far > 0, SIDE + far_count, 2 * SIDE))
        order[slot] = jnp.int32(place)
        near_count += near
        far_count += far
    for slot in range(2 * SIDE):
        place = order[slot]
        lane = pl.multiple_of(remainder(place, dims.blocks) * LANES, LANES)
        value = free_ref[quotient(place, dims.blocks), :, pl.ds(lane, LANES)]
        if slot < SIDE:
            near_ref[slot] = value
        else:
            far_ref[slot - SIDE] = value


def prepare_kernel(
    dims,
    partner_ref,
    iface_ref,
    owner_ref,
    modes_ref,
    inverse_ref,
    take_ref,
    give_ref,
    weight_ref,
    modes_out,
    onehot_out,
    inverse_out,
    partners,
):
    faces = facing(partner_ref, dims)
    row = lax.broadcasted_iota(jnp.int32, (TILE, LANES), 0)
    near_count = jnp.int32(0)
    far_count = jnp.int32(0)
    for place, (near, far, other) in enumerate(faces):
        slot = jnp.where(near > 0, near_count, jnp.where(far > 0, SIDE + far_count, 2 * SIDE))
        partners[slot] = other
        give_ref[place] = jnp.where(row == slot, 1.0, 0.0).astype(F32)
        near_count += near
        far_count += far
    for place, (near, far, other) in enumerate(faces):
        slot_id, block_id = divmod(place, dims.blocks)
        from_near = jnp.int32(0)
        from_far = jnp.int32(SIDE)
        for slot in range(SIDE):
            from_near += (partners[slot] < other).astype(jnp.int32)
            from_far += (partners[SIDE + slot] < other).astype(jnp.int32)
        slot = jnp.where(near > 0, from_near, jnp.where(far > 0, from_far, 2 * SIDE))
        take_ref[place] = jnp.where(row == slot, 1.0, 0.0).astype(F32)
        used = (block_id < iface_ref[slot_id]).astype(F32)
        double = used + jnp.maximum(near, far).astype(F32)
        weight_ref[place] = jnp.where(row == 0, used, double)
    corner_rows = dims.slots * dims.corners
    slot_of_row = quotient(
        lax.broadcasted_iota(jnp.int32, (corner_rows, dims.width), 0), dims.corners
    )
    for slot in range(dims.slots):
        modes = modes_ref[slot].astype(F32)
        stacked = jnp.concatenate([modes] * dims.slots, axis=0)
        modes_out[:, slot * dims.width : (slot + 1) * dims.width] = jnp.where(
            slot_of_row == slot, stacked, 0.0
        ).astype(BF16)
    corner = lax.broadcasted_iota(jnp.int32, (dims.corners, dims.coarse_width), 0)
    column = lax.broadcasted_iota(jnp.int32, (dims.corners, dims.coarse_width), 1)
    hot = []
    for slot in range(dims.slots):
        owners = jnp.zeros((dims.corners, dims.coarse_width), jnp.int32)
        for k in range(dims.corners):
            owners = jnp.where(corner == k, owner_ref[slot, k], owners)
        hot.append(jnp.where(column == owners, 1.0, 0.0).astype(F32))
    onehot = jnp.concatenate(hot, axis=0)
    onehot_out[...] = onehot.astype(BF16)
    inverse_out[...] = lax.dot_general(
        inverse_ref[0],
        onehot,
        (((1,), (1,)), ((), ())),
        precision=lax.Precision.HIGHEST,
        preferred_element_type=F32,
    )


def halves(value):
    high = value.astype(BF16)
    low = (value - high.astype(F32)).astype(BF16)
    return high, low


def lane_sums(value):
    return jnp.sum(value, axis=0, keepdims=True)


def jump_blocks(dims, field_ref, near_ref, far_ref, take_ref, weight_ref):
    for slot in range(dims.slots):
        for block in range(dims.blocks):
            place = slot * dims.blocks + block
            value = block_of(dims, field_ref, slot, block) * weight_ref[place, 0:1, :]
            for side, ref in enumerate((near_ref, far_ref)):
                for j in range(SIDE):
                    row = side * SIDE + j
                    value = value - take_ref[place, row : row + 1, :] * ref[j]
            yield slot, block, value


def coarse_part(dims, high_parts, low_parts, modes_ref, onehot_ref):
    rows = dims.scen
    stacked = jnp.concatenate(
        [jnp.concatenate(high_parts, axis=1), jnp.concatenate(low_parts, axis=1)], axis=0
    )
    sums = lax.dot_general(
        stacked, modes_ref[...], (((1,), (1,)), ((), ())), preferred_element_type=F32
    )
    sums = sums[:rows] + sums[rows:]
    first, rest = halves(sums)
    rest = sums - first.astype(F32)
    second, third = halves(rest)
    pieces = jnp.dot(
        jnp.concatenate([first, second, third], axis=0),
        onehot_ref[...],
        preferred_element_type=F32,
    )
    return pieces[:rows] + pieces[rows : 2 * rows] + pieces[2 * rows :]


def jump_kernel(
    dims,
    field_ref,
    near_ref,
    far_ref,
    take_ref,
    weight_ref,
    modes_ref,
    onehot_ref,
    jump_ref,
    coarse_ref,
):
    high_parts, low_parts = [], []
    for slot, block, value in jump_blocks(
        dims, field_ref, near_ref, far_ref, take_ref, weight_ref
    ):
        jump_ref[slot, :, block * LANES : (block + 1) * LANES] = value
        high, low = halves(value)
        high_parts.append(high)
        low_parts.append(low)
    coarse_ref[...] = coarse_part(dims, high_parts, low_parts, modes_ref, onehot_ref)


def local_kernel(dims, direction_ref, flex_ref, out_ref):
    for slot in range(dims.slots):
        high, low = halves(direction_ref[slot])
        both = jnp.dot(
            jnp.concatenate([high, low], axis=0), flex_ref[slot], preferred_element_type=F32
        )
        out_ref[slot] = both[: dims.scen] + both[dims.scen :]


def add_coarse(dims, local_ref, total, modes_ref, inverse_ref):
    values = jnp.dot(
        total, inverse_ref[...], precision=lax.Precision.HIGHEST, preferred_element_type=F32
    )
    high, low = halves(values)
    both = jnp.dot(
        jnp.concatenate([high, low], axis=0), modes_ref[...], preferred_element_type=F32
    )
    both = both[: dims.scen] + both[dims.scen :]
    return [
        local_ref[slot] + both[:, slot * dims.width : (slot + 1) * dims.width]
        for slot in range(dims.slots)
    ]


def pack(dims, response, give_ref, near_ref, far_ref):
    for side, ref in enumerate((near_ref, far_ref)):
        for j in range(SIDE):
            row = side * SIDE + j
            value = jnp.zeros((dims.scen, LANES), F32)
            for place in range(dims.per_device):
                slot, block = divmod(place, dims.blocks)
                part = response[slot][:, block * LANES : (block + 1) * LANES]
                value = value + give_ref[place, row : row + 1, :] * part
            ref[j] = value


def respond_kernel(
    dims,
    local_ref,
    own_ref,
    other_ref,
    modes_ref,
    inverse_ref,
    give_ref,
    out_ref,
    near_ref,
    far_ref,
):
    response = add_coarse(dims, local_ref, own_ref[...] + other_ref[...], modes_ref, inverse_ref)
    for slot in range(dims.slots):
        out_ref[slot] = response[slot]
    pack(dims, response, give_ref, near_ref, far_ref)


def respond_last_kernel(
    dims,
    local_ref,
    own_ref,
    other_ref,
    modes_ref,
    inverse_ref,
    give_ref,
    weight_ref,
    rhs_ref,
    image_ref,
    out_ref,
    near_ref,
    far_ref,
    sums_ref,
):
    response = add_coarse(dims, local_ref, own_ref[...] + other_ref[...], modes_ref, inverse_ref)
    for slot in range(dims.slots):
        out_ref[slot] = response[slot]
    pack(dims, response, give_ref, near_ref, far_ref)
    zero = jnp.zeros((dims.scen, LANES), F32)
    acc = [zero] * 5
    for slot in range(dims.slots):
        for block in range(dims.blocks):
            place = slot * dims.blocks + block
            rhs = block_of(dims, rhs_ref, slot, block)
            image = block_of(dims, image_ref, slot, block)
            doubled = weight_ref[place, 1:2, :] * response[slot][
                :, block * LANES : (block + 1) * LANES
            ]
            acc[0] = acc[0] + rhs * rhs
            acc[1] = acc[1] + rhs * image
            acc[2] = acc[2] + image * image
            acc[3] = acc[3] + rhs * doubled
            acc[4] = acc[4] + image * doubled
    row = lax.broadcasted_iota(jnp.int32, (TILE, LANES), 0)
    tile = jnp.zeros((TILE, LANES), F32)
    for q in range(5):
        tile = jnp.where(row == q, lane_sums(acc[q]), tile)
    sums_ref[...] = jnp.broadcast_to(tile[None], sums_ref.shape)


def finish_kernel(
    dims,
    sums_ref,
    rhs_ref,
    image_ref,
    field_ref,
    near_ref,
    far_ref,
    take_ref,
    weight_ref,
    multiplier_ref,
    residual_ref,
):
    totals = jnp.sum(jnp.sum(sums_ref[...], axis=0), axis=1, keepdims=True)
    norm, first, square, cross, second = (totals[q : q + 1, :] for q in range(5))
    step = norm / first
    norm_next = norm - 2.0 * step * first + step * step * square
    grown = 1.0 + norm_next / norm
    curve = grown * grown * first - grown * step * (cross + square) + step * step * second
    step_next = norm_next / curve
    on_first = step + step_next * grown
    on_second = step_next * step
    for slot, block, second_image in jump_blocks(
        dims, field_ref, near_ref, far_ref, take_ref, weight_ref
    ):
        lanes = slice(block * LANES, (block + 1) * LANES)
        rhs = rhs_ref[slot, :, lanes]
        image = image_ref[slot, :, lanes]
        multiplier_ref[slot, :, lanes] = on_first * rhs - on_second * image
        residual_ref[slot, :, lanes] = rhs - on_first * image + on_second * second_image


class Dims:
    pass


def call(kernel, dims, outs, args, in_specs=None, out_specs=None, scratch=(), cost=None):
    return pl.pallas_call(
        functools.partial(kernel, dims),
        out_shape=outs,
        in_specs=in_specs if in_specs is not None else [VMEM] * len(args),
        out_specs=out_specs if out_specs is not None else jax.tree.map(lambda _: VMEM, outs),
        scratch_shapes=list(scratch),
        compiler_params=pltpu.CompilerParams(vmem_limit_bytes=16 << 20),
        cost_estimate=cost,
    )(*args)


def local(
    free_response, flexibility, corner_modes, corner_owner, coarse_inverse, iface_blocks, partner
):
    dims = Dims()
    dims.slots, dims.scen, dims.width = free_response.shape
    dims.blocks = partner.shape[1]
    dims.per_device = dims.slots * dims.blocks
    dims.coarse_width = coarse_inverse.shape[1]
    dims.corners = corner_modes.shape[1]
    dims.districts = lax.axis_size("district")
    dims.coarse = lax.axis_size("coarse")
    devices = dims.districts * dims.coarse
    shape = jax.ShapeDtypeStruct
    whole = shape(free_response.shape, F32)
    packed = shape((SIDE, dims.scen, LANES), F32)
    per_block = shape((dims.per_device, TILE, LANES), F32)
    corner_rows = dims.slots * dims.corners

    near_pairs = [(d, d + 1 if d % 2 == 0 else d - 1) for d in range(dims.districts)]
    far_pairs = [
        (d, (d - 1 if d % 2 == 0 else d + 1) % dims.districts) for d in range(dims.districts)
    ]

    def exchange(near, far):
        far = lax.ppermute(far, "district", far_pairs)
        near = lax.ppermute(near, "district", near_pairs)
        return near, far

    def from_group(value):
        if dims.coarse == 2:
            return lax.ppermute(value, "coarse", [(0, 1), (1, 0)])
        return lax.psum(value, "coarse") - value

    near, far = call(
        pack_first_kernel,
        dims,
        (packed, packed),
        (partner, free_response),
        in_specs=[SMEM, VMEM],
        scratch=[pltpu.SMEM((2 * SIDE + 1,), jnp.int32)],
    )
    near, far = exchange(near, far)
    take, give, weight, modes, onehot, inverse = call(
        prepare_kernel,
        dims,
        (
            per_block,
            per_block,
            per_block,
            shape((corner_rows, dims.slots * dims.width), BF16),
            shape((corner_rows, dims.coarse_width), BF16),
            shape((dims.coarse_width, corner_rows), F32),
        ),
        (partner, iface_blocks, corner_owner, corner_modes, coarse_inverse),
        in_specs=[SMEM, SMEM, SMEM, VMEM, VMEM],
        scratch=[pltpu.SMEM((2 * SIDE + 1,), jnp.int32)],
        cost=pl.CostEstimate(flops=10**7, bytes_accessed=10**6, transcendentals=0),
    )

    def jump(field, near, far):
        return call(
            jump_kernel,
            dims,
            (whole, shape((dims.scen, dims.coarse_width), F32)),
            (field, near, far, take, weight, modes, onehot),
        )

    def local_term(direction):
        return call(
            local_kernel,
            dims,
            whole,
            (direction, flexibility),
            cost=pl.CostEstimate(flops=10**7, bytes_accessed=10**6, transcendentals=0),
        )

    rhs, part = jump(free_response, near, far)
    other = from_group(part)
    term = local_term(rhs)
    response, near, far = call(
        respond_kernel,
        dims,
        (whole, packed, packed),
        (term, part, other, modes, inverse, give),
    )
    near, far = exchange(near, far)
    image, part = jump(response, near, far)
    other = from_group(part)
    term = local_term(image)
    response, near, far, sums = call(
        respond_last_kernel,
        dims,
        (whole, packed, packed, shape((devices, TILE, LANES), F32)),
        (term, part, other, modes, inverse, give, weight, rhs, image),
    )
    near, far = exchange(near, far)
    sums = lax.all_to_all(sums, AXES, 0, 0)
    return call(
        finish_kernel,
        dims,
        (whole, whole),
        (sums, rhs, image, response, near, far, take, weight),
    )


def solution(mesh):
    in_specs = (
        P(AXES, None, None),
        P(AXES, None, None),
        P(AXES, None, None),
        P(AXES, None),
        P("district", None, None),
        P(AXES),
        P(AXES, None),
    )
    out_specs = (P(AXES, None, None), P(AXES, None, None))
    return jax.shard_map(local, mesh=mesh, in_specs=in_specs, out_specs=out_specs, check_vma=False)
```

```python
import functools

import jax
import jax.numpy as jnp
from jax import lax
from jax.experimental import pallas as pl
from jax.experimental.pallas import tpu as pltpu
from jax.sharding import PartitionSpec as P


SIDE = 4
AXES = ("district", "coarse")
VMEM = pl.BlockSpec(memory_space=pltpu.VMEM)
HBM = pl.BlockSpec(memory_space=pltpu.MemorySpace.HBM)
F32 = jnp.float32
BF16 = jnp.bfloat16
TILE = 8
LANES = 128


def quotient(value, by):
    if by & (by - 1) == 0:
        return lax.shift_right_logical(value, jnp.int32(by.bit_length() - 1))
    return lax.div(value, jnp.int32(by))


def remainder(value, by):
    if by & (by - 1) == 0:
        return lax.bitwise_and(value, jnp.int32(by - 1))
    return lax.rem(value, jnp.int32(by))


def near_side(index):
    return jnp.where(remainder(index, 2) == 0, index + 1, index - 1)


def far_side(index, count):
    return jnp.where(
        remainder(index, 2) == 0,
        jnp.where(index == 0, count - 1, index - 1),
        jnp.where(index == count - 1, 0, index + 1),
    )


def facing(partner_ref, dims):
    index = lax.axis_index("district")
    near = near_side(index)
    far = far_side(index, dims.districts)
    out = []
    for slot in range(dims.slots):
        for block in range(dims.blocks):
            place = partner_ref[slot, block]
            paired = place >= 0
            safe = jnp.maximum(place, 0)
            district = quotient(safe, dims.coarse * dims.per_device)
            out.append(
                (
                    jnp.logical_and(paired, district == near).astype(jnp.int32),
                    jnp.logical_and(paired, district == far).astype(jnp.int32),
                    remainder(safe, dims.per_device),
                )
            )
    return out


def block_of(ref, slot, block):
    return ref[slot, :, block * LANES : (block + 1) * LANES]


def pack_first_kernel(
    dims, partner_hbm, free_hbm, near_ref, far_ref, free_ref, partner_ref, order, sems
):
    fetch_partner = pltpu.make_async_copy(partner_hbm, partner_ref, sems.at[0])
    fetch_free = pltpu.make_async_copy(free_hbm, free_ref, sems.at[1])
    fetch_partner.start()
    fetch_free.start()
    fetch_partner.wait()
    near_count = jnp.int32(0)
    far_count = jnp.int32(0)
    for place, (near, far, _) in enumerate(facing(partner_ref, dims)):
        slot = jnp.where(near > 0, near_count, jnp.where(far > 0, SIDE + far_count, 2 * SIDE))
        order[slot] = jnp.int32(place)
        near_count += near
        far_count += far
    fetch_free.wait()
    for slot in range(2 * SIDE):
        place = order[slot]
        lane = pl.multiple_of(remainder(place, dims.blocks) * LANES, LANES)
        value = free_ref[quotient(place, dims.blocks), :, pl.ds(lane, LANES)]
        if slot < SIDE:
            near_ref[slot] = value
        else:
            far_ref[slot - SIDE] = value


def prepare_kernel(
    dims,
    partner_hbm,
    iface_hbm,
    owner_hbm,
    modes_hbm,
    inverse_hbm,
    flex_hbm,
    take_ref,
    give_ref,
    weight_ref,
    modes_out,
    onehot_out,
    inverse_out,
    flex_out,
    partner_ref,
    iface_ref,
    owner_ref,
    modes_ref,
    inverse_ref,
    partners,
    sems,
):
    pairs = (
        (partner_hbm, partner_ref),
        (iface_hbm, iface_ref),
        (owner_hbm, owner_ref),
        (modes_hbm, modes_ref),
        (inverse_hbm, inverse_ref),
        (flex_hbm, flex_out),
    )
    fetches = [
        pltpu.make_async_copy(there, here, sems.at[i]) for i, (there, here) in enumerate(pairs)
    ]
    for fetch in fetches:
        fetch.start()
    for fetch in fetches[:-1]:
        fetch.wait()
    faces = facing(partner_ref, dims)
    row = lax.broadcasted_iota(jnp.int32, (TILE, LANES), 0)
    near_count = jnp.int32(0)
    far_count = jnp.int32(0)
    for place, (near, far, other) in enumerate(faces):
        slot = jnp.where(near > 0, near_count, jnp.where(far > 0, SIDE + far_count, 2 * SIDE))
        partners[slot] = other
        give_ref[place] = jnp.where(row == slot, 1.0, 0.0).astype(F32)
        near_count += near
        far_count += far
    for place, (near, far, other) in enumerate(faces):
        slot_id, block_id = divmod(place, dims.blocks)
        from_near = jnp.int32(0)
        from_far = jnp.int32(SIDE)
        for slot in range(SIDE):
            from_near += (partners[slot] < other).astype(jnp.int32)
            from_far += (partners[SIDE + slot] < other).astype(jnp.int32)
        slot = jnp.where(near > 0, from_near, jnp.where(far > 0, from_far, 2 * SIDE))
        take_ref[place] = jnp.where(row == slot, 1.0, 0.0).astype(F32)
        used = (block_id < iface_ref[slot_id]).astype(F32)
        double = used + jnp.maximum(near, far).astype(F32)
        weight_ref[place] = jnp.where(row == 0, used, double)
    corner_rows = dims.slots * dims.corners
    slot_of_row = quotient(
        lax.broadcasted_iota(jnp.int32, (corner_rows, dims.width), 0), dims.corners
    )
    for slot in range(dims.slots):
        modes = modes_ref[slot].astype(F32)
        stacked = jnp.concatenate([modes] * dims.slots, axis=0)
        modes_out[:, slot * dims.width : (slot + 1) * dims.width] = jnp.where(
            slot_of_row == slot, stacked, 0.0
        ).astype(BF16)
    corner = lax.broadcasted_iota(jnp.int32, (dims.corners, dims.coarse_width), 0)
    column = lax.broadcasted_iota(jnp.int32, (dims.corners, dims.coarse_width), 1)
    hot = []
    for slot in range(dims.slots):
        owners = jnp.zeros((dims.corners, dims.coarse_width), jnp.int32)
        for k in range(dims.corners):
            owners = jnp.where(corner == k, owner_ref[slot, k], owners)
        hot.append(jnp.where(column == owners, 1.0, 0.0).astype(F32))
    onehot = jnp.concatenate(hot, axis=0)
    onehot_out[...] = onehot.astype(BF16)
    inverse_out[...] = lax.dot_general(
        inverse_ref[0],
        onehot,
        (((1,), (1,)), ((), ())),
        precision=lax.Precision.HIGHEST,
        preferred_element_type=F32,
    )
    fetches[-1].wait()


def halves(value):
    high = value.astype(BF16)
    low = (value - high.astype(F32)).astype(BF16)
    return high, low


def lane_sums(value):
    return jnp.sum(value, axis=0, keepdims=True)


def jump_blocks(dims, field_ref, near_ref, far_ref, take_ref, weight_ref):
    for slot in range(dims.slots):
        for block in range(dims.blocks):
            place = slot * dims.blocks + block
            value = block_of(field_ref, slot, block) * weight_ref[place, 0:1, :]
            for side, ref in enumerate((near_ref, far_ref)):
                for j in range(SIDE):
                    row = side * SIDE + j
                    value = value - take_ref[place, row : row + 1, :] * ref[j]
            yield slot, block, value


def coarse_part(dims, high_parts, low_parts, modes_ref, onehot_ref):
    rows = dims.scen
    stacked = jnp.concatenate(
        [jnp.concatenate(high_parts, axis=1), jnp.concatenate(low_parts, axis=1)], axis=0
    )
    sums = lax.dot_general(
        stacked, modes_ref[...], (((1,), (1,)), ((), ())), preferred_element_type=F32
    )
    sums = sums[:rows] + sums[rows:]
    first, rest = halves(sums)
    rest = sums - first.astype(F32)
    second, third = halves(rest)
    pieces = jnp.dot(
        jnp.concatenate([first, second, third], axis=0),
        onehot_ref[...],
        preferred_element_type=F32,
    )
    return pieces[:rows] + pieces[rows : 2 * rows] + pieces[2 * rows :]


def jump_kernel(
    dims,
    field_ref,
    near_ref,
    far_ref,
    take_ref,
    weight_ref,
    modes_ref,
    onehot_ref,
    jump_ref,
    coarse_ref,
):
    high_parts, low_parts = [], []
    for slot, block, value in jump_blocks(
        dims, field_ref, near_ref, far_ref, take_ref, weight_ref
    ):
        jump_ref[slot, :, block * LANES : (block + 1) * LANES] = value
        high, low = halves(value)
        high_parts.append(high)
        low_parts.append(low)
    coarse_ref[...] = coarse_part(dims, high_parts, low_parts, modes_ref, onehot_ref)


def local_kernel(dims, direction_ref, flex_ref, out_ref):
    for slot in range(dims.slots):
        high, low = halves(direction_ref[slot])
        both = jnp.dot(
            jnp.concatenate([high, low], axis=0), flex_ref[slot], preferred_element_type=F32
        )
        out_ref[slot] = both[: dims.scen] + both[dims.scen :]


def local_last_kernel(dims, direction_ref, flex_ref, rhs_ref, out_ref, sums_ref):
    local_kernel(dims, direction_ref, flex_ref, out_ref)
    acc = [jnp.zeros((dims.scen, LANES), F32)] * 3
    for slot in range(dims.slots):
        for block in range(dims.blocks):
            rhs = block_of(rhs_ref, slot, block)
            image = block_of(direction_ref, slot, block)
            acc[0] = acc[0] + rhs * rhs
            acc[1] = acc[1] + rhs * image
            acc[2] = acc[2] + image * image
    sums_ref[...] = rows_of(acc, 0)


def rows_of(parts, first):
    row = lax.broadcasted_iota(jnp.int32, (TILE, LANES), 0)
    tile = jnp.zeros((TILE, LANES), F32)
    for q, part in enumerate(parts):
        tile = jnp.where(row == first + q, lane_sums(part), tile)
    return tile


def add_coarse(dims, local_ref, total, modes_ref, inverse_ref):
    values = jnp.dot(
        total, inverse_ref[...], precision=lax.Precision.HIGHEST, preferred_element_type=F32
    )
    high, low = halves(values)
    both = jnp.dot(
        jnp.concatenate([high, low], axis=0), modes_ref[...], preferred_element_type=F32
    )
    both = both[: dims.scen] + both[dims.scen :]
    return [
        local_ref[slot] + both[:, slot * dims.width : (slot + 1) * dims.width]
        for slot in range(dims.slots)
    ]


def pack(dims, response, give_ref, near_ref, far_ref):
    for side, ref in enumerate((near_ref, far_ref)):
        for j in range(SIDE):
            row = side * SIDE + j
            value = jnp.zeros((dims.scen, LANES), F32)
            for place in range(dims.per_device):
                slot, block = divmod(place, dims.blocks)
                part = response[slot][:, block * LANES : (block + 1) * LANES]
                value = value + give_ref[place, row : row + 1, :] * part
            ref[j] = value


def respond_kernel(
    dims,
    local_ref,
    own_ref,
    other_ref,
    modes_ref,
    inverse_ref,
    give_ref,
    out_ref,
    near_ref,
    far_ref,
):
    response = add_coarse(dims, local_ref, own_ref[...] + other_ref[...], modes_ref, inverse_ref)
    for slot in range(dims.slots):
        out_ref[slot] = response[slot]
    pack(dims, response, give_ref, near_ref, far_ref)


def respond_last_kernel(
    dims,
    local_ref,
    own_ref,
    other_ref,
    modes_ref,
    inverse_ref,
    give_ref,
    weight_ref,
    rhs_ref,
    image_ref,
    early_ref,
    out_ref,
    near_ref,
    far_ref,
    sums_ref,
):
    response = add_coarse(dims, local_ref, own_ref[...] + other_ref[...], modes_ref, inverse_ref)
    acc = [jnp.zeros((dims.scen, LANES), F32)] * 2
    for slot in range(dims.slots):
        out_ref[slot] = response[slot]
        for block in range(dims.blocks):
            place = slot * dims.blocks + block
            doubled = weight_ref[place, 1:2, :] * response[slot][
                :, block * LANES : (block + 1) * LANES
            ]
            acc[0] = acc[0] + block_of(rhs_ref, slot, block) * doubled
            acc[1] = acc[1] + block_of(image_ref, slot, block) * doubled
    sums_ref[...] = jnp.broadcast_to((early_ref[...] + rows_of(acc, 3))[None], sums_ref.shape)
    pack(dims, response, give_ref, near_ref, far_ref)


def finish_kernel(
    dims,
    sums_ref,
    rhs_ref,
    image_ref,
    field_ref,
    near_ref,
    far_ref,
    take_ref,
    weight_ref,
    multiplier_ref,
    residual_ref,
):
    totals = jnp.sum(jnp.sum(sums_ref[...], axis=0), axis=1, keepdims=True)
    norm, first, square, cross, second = (totals[q : q + 1, :] for q in range(5))
    step = norm / first
    norm_next = norm - 2.0 * step * first + step * step * square
    grown = 1.0 + norm_next / norm
    curve = grown * grown * first - grown * step * (cross + square) + step * step * second
    step_next = norm_next / curve
    on_first = step + step_next * grown
    on_second = step_next * step
    for slot, block, second_image in jump_blocks(
        dims, field_ref, near_ref, far_ref, take_ref, weight_ref
    ):
        lanes = slice(block * LANES, (block + 1) * LANES)
        rhs = rhs_ref[slot, :, lanes]
        image = image_ref[slot, :, lanes]
        multiplier_ref[slot, :, lanes] = on_first * rhs - on_second * image
        residual_ref[slot, :, lanes] = rhs - on_first * image + on_second * second_image


class Dims:
    pass


def stay(value):
    return pltpu.with_memory_space_constraint(value, pltpu.MemorySpace.HBM)


def call(kernel, dims, outs, args, in_specs=None, out_specs=None, scratch=(), cost=None):
    return pl.pallas_call(
        functools.partial(kernel, dims),
        out_shape=outs,
        in_specs=in_specs if in_specs is not None else [VMEM] * len(args),
        out_specs=out_specs if out_specs is not None else jax.tree.map(lambda _: VMEM, outs),
        scratch_shapes=list(scratch),
        compiler_params=pltpu.CompilerParams(vmem_limit_bytes=16 << 20),
        cost_estimate=cost,
    )(*args)


def local(
    free_response, flexibility, corner_modes, corner_owner, coarse_inverse, iface_blocks, partner
):
    dims = Dims()
    dims.slots, dims.scen, dims.width = free_response.shape
    dims.blocks = partner.shape[1]
    dims.per_device = dims.slots * dims.blocks
    dims.coarse_width = coarse_inverse.shape[1]
    dims.corners = corner_modes.shape[1]
    dims.districts = lax.axis_size("district")
    dims.coarse = lax.axis_size("coarse")
    devices = dims.districts * dims.coarse
    shape = jax.ShapeDtypeStruct
    whole = shape(free_response.shape, F32)
    packed = shape((SIDE, dims.scen, LANES), F32)
    per_block = shape((dims.per_device, TILE, LANES), F32)
    corner_rows = dims.slots * dims.corners

    near_pairs = [(d, d + 1 if d % 2 == 0 else d - 1) for d in range(dims.districts)]
    far_pairs = [
        (d, (d - 1 if d % 2 == 0 else d + 1) % dims.districts) for d in range(dims.districts)
    ]

    def exchange(near, far):
        far = lax.ppermute(far, "district", far_pairs)
        near = lax.ppermute(near, "district", near_pairs)
        return near, far

    def from_group(value):
        if dims.coarse == 2:
            return lax.ppermute(value, "coarse", [(0, 1), (1, 0)])
        return lax.psum(value, "coarse") - value

    near, far, field = call(
        pack_first_kernel,
        dims,
        (packed, packed, whole),
        (stay(partner), stay(free_response)),
        in_specs=[HBM, HBM],
        scratch=[
            pltpu.SMEM(partner.shape, jnp.int32),
            pltpu.SMEM((2 * SIDE + 1,), jnp.int32),
            pltpu.SemaphoreType.DMA((2,)),
        ],
    )
    near, far = exchange(near, far)
    take, give, weight, modes, onehot, inverse, flex = call(
        prepare_kernel,
        dims,
        (
            per_block,
            per_block,
            per_block,
            shape((corner_rows, dims.slots * dims.width), BF16),
            shape((corner_rows, dims.coarse_width), BF16),
            shape((dims.coarse_width, corner_rows), F32),
            shape(flexibility.shape, BF16),
        ),
        tuple(
            stay(value)
            for value in (
                partner,
                iface_blocks,
                corner_owner,
                corner_modes,
                coarse_inverse,
                flexibility,
            )
        ),
        in_specs=[HBM] * 6,
        scratch=[
            pltpu.SMEM(partner.shape, jnp.int32),
            pltpu.SMEM(iface_blocks.shape, jnp.int32),
            pltpu.SMEM(corner_owner.shape, jnp.int32),
            pltpu.VMEM(corner_modes.shape, BF16),
            pltpu.VMEM(coarse_inverse.shape, F32),
            pltpu.SMEM((2 * SIDE + 1,), jnp.int32),
            pltpu.SemaphoreType.DMA((6,)),
        ],
        cost=pl.CostEstimate(flops=10**7, bytes_accessed=4 * 10**6, transcendentals=0),
    )

    def jump(field, near, far):
        return call(
            jump_kernel,
            dims,
            (whole, shape((dims.scen, dims.coarse_width), F32)),
            (field, near, far, take, weight, modes, onehot),
        )

    matmul_cost = pl.CostEstimate(flops=10**8, bytes_accessed=3 * 10**6, transcendentals=0)
    rhs, part = jump(field, near, far)
    other = from_group(part)
    term = call(local_kernel, dims, whole, (rhs, flex), cost=matmul_cost)
    response, near, far = call(
        respond_kernel,
        dims,
        (whole, packed, packed),
        (term, part, other, modes, inverse, give),
    )
    near, far = exchange(near, far)
    image, part = jump(response, near, far)
    other = from_group(part)
    term, early = call(
        local_last_kernel,
        dims,
        (whole, shape((TILE, LANES), F32)),
        (image, flex, rhs),
        cost=matmul_cost,
    )
    response, near, far, sums = call(
        respond_last_kernel,
        dims,
        (whole, packed, packed, shape((devices, TILE, LANES), F32)),
        (term, part, other, modes, inverse, give, weight, rhs, image, early),
    )
    sums = lax.all_to_all(sums, AXES, 0, 0)
    near, far = exchange(near, far)
    return call(
        finish_kernel,
        dims,
        (whole, whole),
        (sums, rhs, image, response, near, far, take, weight),
    )


def solution(mesh):
    in_specs = (
        P(AXES, None, None),
        P(AXES, None, None),
        P(AXES, None, None),
        P(AXES, None),
        P("district", None, None),
        P(AXES),
        P(AXES, None),
    )
    out_specs = (P(AXES, None, None), P(AXES, None, None))
    return jax.shard_map(local, mesh=mesh, in_specs=in_specs, out_specs=out_specs, check_vma=False)
```

```python
import functools

import jax
import jax.numpy as jnp
from jax import lax
from jax.experimental import pallas as pl
from jax.experimental.pallas import tpu as pltpu
from jax.sharding import PartitionSpec as P


SIDE = 4
AXES = ("district", "coarse")
VMEM = pl.BlockSpec(memory_space=pltpu.VMEM)
HBM = pl.BlockSpec(memory_space=pltpu.MemorySpace.HBM)
F32 = jnp.float32
BF16 = jnp.bfloat16
TILE = 8
LANES = 128


def quotient(value, by):
    if by & (by - 1) == 0:
        return lax.shift_right_logical(value, jnp.int32(by.bit_length() - 1))
    return lax.div(value, jnp.int32(by))


def remainder(value, by):
    if by & (by - 1) == 0:
        return lax.bitwise_and(value, jnp.int32(by - 1))
    return lax.rem(value, jnp.int32(by))


def near_side(index):
    return jnp.where(remainder(index, 2) == 0, index + 1, index - 1)


def far_side(index, count):
    return jnp.where(
        remainder(index, 2) == 0,
        jnp.where(index == 0, count - 1, index - 1),
        jnp.where(index == count - 1, 0, index + 1),
    )


def facing(partner_ref, dims):
    index = lax.axis_index("district")
    near = near_side(index)
    far = far_side(index, dims.districts)
    out = []
    for slot in range(dims.slots):
        for block in range(dims.blocks):
            place = partner_ref[slot, block]
            paired = place >= 0
            safe = jnp.maximum(place, 0)
            district = quotient(safe, dims.coarse * dims.per_device)
            out.append(
                (
                    jnp.logical_and(paired, district == near).astype(jnp.int32),
                    jnp.logical_and(paired, district == far).astype(jnp.int32),
                    remainder(safe, dims.per_device),
                )
            )
    return out


def block_of(ref, slot, block):
    return ref[slot, :, block * LANES : (block + 1) * LANES]


def pack_first_kernel(
    dims, partner_hbm, free_hbm, near_ref, far_ref, free_ref, partner_ref, order, sems
):
    fetch_partner = pltpu.make_async_copy(partner_hbm, partner_ref, sems.at[0])
    fetch_free = [
        pltpu.make_async_copy(free_hbm.at[slot], free_ref.at[slot], sems.at[1 + slot])
        for slot in range(dims.slots)
    ]
    fetch_partner.start()
    for fetch in fetch_free:
        fetch.start()
    fetch_partner.wait()
    near_count = jnp.int32(0)
    far_count = jnp.int32(0)
    for place, (near, far, _) in enumerate(facing(partner_ref, dims)):
        slot = jnp.where(near > 0, near_count, jnp.where(far > 0, SIDE + far_count, 2 * SIDE))
        order[slot] = jnp.int32(place)
        near_count += near
        far_count += far
    for fetch in fetch_free:
        fetch.wait()
    for slot in range(2 * SIDE):
        place = order[slot]
        lane = pl.multiple_of(remainder(place, dims.blocks) * LANES, LANES)
        value = free_ref[quotient(place, dims.blocks), :, pl.ds(lane, LANES)]
        if slot < SIDE:
            near_ref[slot] = value
        else:
            far_ref[slot - SIDE] = value


def prepare_kernel(
    dims,
    partner_hbm,
    iface_hbm,
    owner_hbm,
    modes_hbm,
    inverse_hbm,
    flex_hbm,
    others_in,
    take_ref,
    give_ref,
    weight_ref,
    modes_out,
    high_out,
    low_out,
    flex_out,
    partner_ref,
    iface_ref,
    owner_ref,
    modes_ref,
    inverse_ref,
    others_ref,
    partners,
    sems,
):
    pairs = (
        (partner_hbm, partner_ref),
        (iface_hbm, iface_ref),
        (owner_hbm, owner_ref),
        (others_in, others_ref),
        (modes_hbm, modes_ref),
        (inverse_hbm, inverse_ref),
        (flex_hbm, flex_out),
    )
    fetches = [
        pltpu.make_async_copy(there, here, sems.at[i]) for i, (there, here) in enumerate(pairs)
    ]
    for fetch in fetches:
        fetch.start()
    for fetch in fetches[:-1]:
        fetch.wait()
    faces = facing(partner_ref, dims)
    row = lax.broadcasted_iota(jnp.int32, (TILE, LANES), 0)
    near_count = jnp.int32(0)
    far_count = jnp.int32(0)
    for place, (near, far, other) in enumerate(faces):
        slot = jnp.where(near > 0, near_count, jnp.where(far > 0, SIDE + far_count, 2 * SIDE))
        partners[slot] = other
        give_ref[place] = jnp.where(row == slot, 1.0, 0.0).astype(F32)
        near_count += near
        far_count += far
    for place, (near, far, other) in enumerate(faces):
        slot_id, block_id = divmod(place, dims.blocks)
        from_near = jnp.int32(0)
        from_far = jnp.int32(SIDE)
        for slot in range(SIDE):
            from_near += (partners[slot] < other).astype(jnp.int32)
            from_far += (partners[SIDE + slot] < other).astype(jnp.int32)
        slot = jnp.where(near > 0, from_near, jnp.where(far > 0, from_far, 2 * SIDE))
        take_ref[place] = jnp.where(row == slot, 1.0, 0.0).astype(F32)
        used = (block_id < iface_ref[slot_id]).astype(F32)
        double = used + jnp.maximum(near, far).astype(F32)
        weight_ref[place] = jnp.where(row == 0, used, double)
    member = lax.axis_index("coarse")
    all_slots = dims.slots * dims.coarse
    corner_rows = all_slots * dims.corners
    slot_of_row = quotient(
        lax.broadcasted_iota(jnp.int32, (corner_rows, dims.width), 0), dims.corners
    )
    placed = []
    for slot in range(dims.slots):
        modes = modes_ref[slot].astype(F32)
        stacked = jnp.concatenate([modes] * all_slots, axis=0)
        block = jnp.where(slot_of_row == member * dims.slots + slot, stacked, 0.0).astype(BF16)
        modes_out[:, slot * dims.width : (slot + 1) * dims.width] = block
        placed.append(block)
    corner = lax.broadcasted_iota(jnp.int32, (dims.corners, dims.coarse_width), 0)
    column = lax.broadcasted_iota(jnp.int32, (dims.corners, dims.coarse_width), 1)
    hot, own_hot = [], []
    for place in range(all_slots):
        who, slot = divmod(place, dims.slots)
        owners = jnp.zeros((dims.corners, dims.coarse_width), jnp.int32)
        for k in range(dims.corners):
            if dims.coarse == 2:
                owner = jnp.where(member == who, owner_ref[slot, k], others_ref[slot, k])
            else:
                owner = others_ref[who, slot, k]
            owners = jnp.where(corner == k, owner, owners)
        hot.append(jnp.where(column == owners, 1.0, 0.0).astype(F32))
        own_hot.append(jnp.where(member == who, hot[-1], 0.0))
    onto = jnp.dot(
        jnp.concatenate(hot, axis=0),
        inverse_ref[0],
        precision=lax.Precision.HIGHEST,
        preferred_element_type=F32,
    )
    between = lax.dot_general(
        onto,
        jnp.concatenate(own_hot, axis=0),
        (((1,), (1,)), ((), ())),
        precision=lax.Precision.HIGHEST,
        preferred_element_type=F32,
    )
    pieces = jnp.concatenate(thirds(between), axis=0)
    for slot in range(dims.slots):
        lanes = slice(slot * dims.width, (slot + 1) * dims.width)
        spread = jnp.dot(pieces, placed[slot], preferred_element_type=F32)
        spread = (
            spread[:corner_rows]
            + spread[corner_rows : 2 * corner_rows]
            + spread[2 * corner_rows :]
        )
        high, low = halves(spread)
        high_out[:, lanes] = high
        low_out[:, lanes] = low
    fetches[-1].wait()


def halves(value):
    high = value.astype(BF16)
    low = (value - high.astype(F32)).astype(BF16)
    return high, low


def thirds(value):
    first = value.astype(BF16)
    rest = value - first.astype(F32)
    second, third = halves(rest)
    return first, second, third


def lane_sums(value):
    return jnp.sum(value, axis=0, keepdims=True)


def jump_blocks(dims, field_ref, near_ref, far_ref, take_ref, weight_ref):
    for slot in range(dims.slots):
        for block in range(dims.blocks):
            place = slot * dims.blocks + block
            value = block_of(field_ref, slot, block) * weight_ref[place, 0:1, :]
            for side, ref in enumerate((near_ref, far_ref)):
                for j in range(SIDE):
                    row = side * SIDE + j
                    value = value - take_ref[place, row : row + 1, :] * ref[j]
            yield slot, block, value


def corner_sums(dims, high_parts, low_parts, modes_ref):
    stacked = jnp.concatenate(
        [jnp.concatenate(high_parts, axis=1), jnp.concatenate(low_parts, axis=1)], axis=0
    )
    sums = lax.dot_general(
        stacked, modes_ref[...], (((1,), (1,)), ((), ())), preferred_element_type=F32
    )
    return sums[: dims.scen] + sums[dims.scen :]


def jump_kernel(
    dims,
    field_ref,
    near_ref,
    far_ref,
    take_ref,
    weight_ref,
    modes_ref,
    jump_ref,
    corner_ref,
):
    high_parts, low_parts = [], []
    for slot, block, value in jump_blocks(
        dims, field_ref, near_ref, far_ref, take_ref, weight_ref
    ):
        jump_ref[slot, :, block * LANES : (block + 1) * LANES] = value
        high, low = halves(value)
        high_parts.append(high)
        low_parts.append(low)
    corner_ref[...] = corner_sums(dims, high_parts, low_parts, modes_ref)


def local_kernel(dims, direction_ref, flex_ref, out_ref):
    for slot in range(dims.slots):
        high, low = halves(direction_ref[slot])
        both = jnp.dot(
            jnp.concatenate([high, low], axis=0), flex_ref[slot], preferred_element_type=F32
        )
        out_ref[slot] = both[: dims.scen] + both[dims.scen :]


def local_last_kernel(dims, direction_ref, flex_ref, rhs_ref, out_ref, sums_ref):
    local_kernel(dims, direction_ref, flex_ref, out_ref)
    acc = [jnp.zeros((dims.scen, LANES), F32)] * 3
    for slot in range(dims.slots):
        for block in range(dims.blocks):
            rhs = block_of(rhs_ref, slot, block)
            image = block_of(direction_ref, slot, block)
            acc[0] = acc[0] + rhs * rhs
            acc[1] = acc[1] + rhs * image
            acc[2] = acc[2] + image * image
    sums_ref[...] = rows_of(acc, 0)


def rows_of(parts, first):
    row = lax.broadcasted_iota(jnp.int32, (TILE, LANES), 0)
    tile = jnp.zeros((TILE, LANES), F32)
    for q, part in enumerate(parts):
        tile = jnp.where(row == first + q, lane_sums(part), tile)
    return tile


def on_diagonal():
    row = lax.broadcasted_iota(jnp.int32, (TILE, LANES), 0)
    return row == lax.broadcasted_iota(jnp.int32, (TILE, LANES), 1)


def add_coarse(dims, local_ref, sums, high_ref, low_ref):
    high, low = halves(sums)
    both = jnp.concatenate([high, low], axis=0)
    for slot in range(dims.slots):
        lanes = slice(slot * dims.width, (slot + 1) * dims.width)
        part = jnp.dot(both, high_ref[:, lanes], preferred_element_type=F32)
        rest = jnp.dot(high, low_ref[:, lanes], preferred_element_type=F32)
        yield local_ref[slot] + (part[: dims.scen] + part[dims.scen :] + rest)


def pack(dims, response, give_ref, near_ref, far_ref):
    for side, ref in enumerate((near_ref, far_ref)):
        for j in range(SIDE):
            row = side * SIDE + j
            value = jnp.zeros((dims.scen, LANES), F32)
            for place in range(dims.per_device):
                slot, block = divmod(place, dims.blocks)
                part = response[slot][:, block * LANES : (block + 1) * LANES]
                value = value + give_ref[place, row : row + 1, :] * part
            ref[j] = value


def respond_kernel(
    dims,
    local_ref,
    own_ref,
    other_ref,
    high_ref,
    low_ref,
    give_ref,
    out_ref,
    near_ref,
    far_ref,
):
    response = list(add_coarse(dims, local_ref, own_ref[...] + other_ref[...], high_ref, low_ref))
    for slot in range(dims.slots):
        out_ref[slot] = response[slot]
    pack(dims, response, give_ref, near_ref, far_ref)


def respond_last_kernel(
    dims,
    local_ref,
    own_ref,
    other_ref,
    high_ref,
    low_ref,
    give_ref,
    weight_ref,
    rhs_ref,
    image_ref,
    early_ref,
    out_ref,
    near_ref,
    far_ref,
    sums_hbm,
    sums_ref,
    sem,
):
    response = list(add_coarse(dims, local_ref, own_ref[...] + other_ref[...], high_ref, low_ref))
    acc = [jnp.zeros((dims.scen, LANES), F32)] * 2
    for slot in range(dims.slots):
        for block in range(dims.blocks):
            place = slot * dims.blocks + block
            doubled = weight_ref[place, 1:2, :] * response[slot][
                :, block * LANES : (block + 1) * LANES
            ]
            acc[0] = acc[0] + block_of(rhs_ref, slot, block) * doubled
            acc[1] = acc[1] + block_of(image_ref, slot, block) * doubled
    totals = jnp.sum(early_ref[...] + rows_of(acc, 3), axis=1, keepdims=True)
    sums_ref[...] = jnp.broadcast_to(
        lane_sums(jnp.where(on_diagonal(), totals, 0.0))[None], sums_ref.shape
    )
    put = pltpu.make_async_copy(sums_ref, sums_hbm, sem)
    put.start()
    for slot in range(dims.slots):
        out_ref[slot] = response[slot]
    pack(dims, response, give_ref, near_ref, far_ref)
    put.wait()


def finish_kernel(
    dims,
    sums_ref,
    rhs_ref,
    image_ref,
    field_ref,
    near_ref,
    far_ref,
    take_ref,
    weight_ref,
    multiplier_hbm,
    residual_hbm,
    multiplier_ref,
    residual_ref,
    sems,
):
    row = jnp.sum(sums_ref[...], axis=0)
    totals = jnp.sum(jnp.where(on_diagonal(), row, 0.0), axis=1, keepdims=True)
    norm, first, square, cross, second = (totals[q : q + 1, :] for q in range(5))
    step = norm / first
    norm_next = norm - 2.0 * step * first + step * step * square
    grown = 1.0 + norm_next / norm
    curve = grown * grown * first - grown * step * (cross + square) + step * step * second
    step_next = norm_next / curve
    on_first = step + step_next * grown
    on_second = step_next * step
    puts = []
    for slot, block, second_image in jump_blocks(
        dims, field_ref, near_ref, far_ref, take_ref, weight_ref
    ):
        lanes = slice(block * LANES, (block + 1) * LANES)
        rhs = rhs_ref[slot, :, lanes]
        image = image_ref[slot, :, lanes]
        multiplier_ref[slot, :, lanes] = on_first * rhs - on_second * image
        residual_ref[slot, :, lanes] = rhs - on_first * image + on_second * second_image
        if block + 1 == dims.blocks:
            for i, (here, there) in enumerate(
                ((multiplier_ref, multiplier_hbm), (residual_ref, residual_hbm))
            ):
                put = pltpu.make_async_copy(here.at[slot], there.at[slot], sems.at[i, slot])
                put.start()
                puts.append(put)
    for put in puts:
        put.wait()


class Dims:
    pass


def stay(value):
    return pltpu.with_memory_space_constraint(value, pltpu.MemorySpace.HBM)


def call(kernel, dims, outs, args, in_specs=None, out_specs=None, scratch=(), cost=None):
    return pl.pallas_call(
        functools.partial(kernel, dims),
        out_shape=outs,
        in_specs=in_specs if in_specs is not None else [VMEM] * len(args),
        out_specs=out_specs if out_specs is not None else jax.tree.map(lambda _: VMEM, outs),
        scratch_shapes=list(scratch),
        compiler_params=pltpu.CompilerParams(vmem_limit_bytes=16 << 20),
        cost_estimate=cost,
    )(*args)


def local(
    free_response, flexibility, corner_modes, corner_owner, coarse_inverse, iface_blocks, partner
):
    dims = Dims()
    dims.slots, dims.scen, dims.width = free_response.shape
    dims.blocks = partner.shape[1]
    dims.per_device = dims.slots * dims.blocks
    dims.coarse_width = coarse_inverse.shape[1]
    dims.corners = corner_modes.shape[1]
    dims.districts = lax.axis_size("district")
    dims.coarse = lax.axis_size("coarse")
    devices = dims.districts * dims.coarse
    shape = jax.ShapeDtypeStruct
    whole = shape(free_response.shape, F32)
    packed = shape((SIDE, dims.scen, LANES), F32)
    per_block = shape((dims.per_device, TILE, LANES), F32)
    corner_rows = dims.slots * dims.corners * dims.coarse

    near_pairs = [(d, d + 1 if d % 2 == 0 else d - 1) for d in range(dims.districts)]
    far_pairs = [
        (d, (d - 1 if d % 2 == 0 else d + 1) % dims.districts) for d in range(dims.districts)
    ]

    def exchange(near, far):
        far = lax.ppermute(far, "district", far_pairs)
        near = lax.ppermute(near, "district", near_pairs)
        return near, far

    def from_group(value):
        if dims.coarse == 2:
            return lax.ppermute(value, "coarse", [(0, 1), (1, 0)])
        return lax.psum(value, "coarse") - value

    near, far, field = call(
        pack_first_kernel,
        dims,
        (packed, packed, whole),
        (stay(partner), stay(free_response)),
        in_specs=[HBM, HBM],
        scratch=[
            pltpu.SMEM(partner.shape, jnp.int32),
            pltpu.SMEM((2 * SIDE + 1,), jnp.int32),
            pltpu.SemaphoreType.DMA((1 + dims.slots,)),
        ],
    )
    near, far = exchange(near, far)
    if dims.coarse == 2:
        others = lax.ppermute(corner_owner, "coarse", [(0, 1), (1, 0)])
    else:
        others = lax.all_gather(corner_owner, "coarse")
    take, give, weight, modes, high, low, flex = call(
        prepare_kernel,
        dims,
        (
            per_block,
            per_block,
            per_block,
            shape((corner_rows, dims.slots * dims.width), BF16),
            shape((corner_rows, dims.slots * dims.width), BF16),
            shape((corner_rows, dims.slots * dims.width), BF16),
            shape(flexibility.shape, BF16),
        ),
        tuple(
            stay(value)
            for value in (
                partner,
                iface_blocks,
                corner_owner,
                corner_modes,
                coarse_inverse,
                flexibility,
            )
        )
        + (others,),
        in_specs=[HBM] * 6 + [VMEM],
        scratch=[
            pltpu.SMEM(partner.shape, jnp.int32),
            pltpu.SMEM(iface_blocks.shape, jnp.int32),
            pltpu.SMEM(corner_owner.shape, jnp.int32),
            pltpu.VMEM(corner_modes.shape, BF16),
            pltpu.VMEM(coarse_inverse.shape, F32),
            pltpu.SMEM(others.shape, jnp.int32),
            pltpu.SMEM((2 * SIDE + 1,), jnp.int32),
            pltpu.SemaphoreType.DMA((7,)),
        ],
        cost=pl.CostEstimate(flops=10**7, bytes_accessed=4 * 10**6, transcendentals=0),
    )

    def jump(field, near, far):
        return call(
            jump_kernel,
            dims,
            (whole, shape((dims.scen, corner_rows), F32)),
            (field, near, far, take, weight, modes),
        )

    matmul_cost = pl.CostEstimate(flops=10**8, bytes_accessed=3 * 10**6, transcendentals=0)
    rhs, part = jump(field, near, far)
    other = from_group(part)
    term = call(local_kernel, dims, whole, (rhs, flex), cost=matmul_cost)
    response, near, far = call(
        respond_kernel,
        dims,
        (whole, packed, packed),
        (term, part, other, high, low, give),
    )
    near, far = exchange(near, far)
    image, part = jump(response, near, far)
    other = from_group(part)
    term, early = call(
        local_last_kernel,
        dims,
        (whole, shape((TILE, LANES), F32)),
        (image, flex, rhs),
        cost=matmul_cost,
    )
    response, near, far, sums = call(
        respond_last_kernel,
        dims,
        (whole, packed, packed, shape((devices, 1, LANES), F32)),
        (term, part, other, high, low, give, weight, rhs, image, early),
        out_specs=(VMEM, VMEM, VMEM, HBM),
        scratch=[pltpu.VMEM((devices, 1, LANES), F32), pltpu.SemaphoreType.DMA],
    )
    sums = lax.all_to_all(sums, AXES, 0, 0)
    near, far = exchange(near, far)
    return call(
        finish_kernel,
        dims,
        (whole, whole),
        (sums, rhs, image, response, near, far, take, weight),
        out_specs=(HBM, HBM),
        scratch=[
            pltpu.VMEM(free_response.shape, F32),
            pltpu.VMEM(free_response.shape, F32),
            pltpu.SemaphoreType.DMA((2, dims.slots)),
        ],
    )


def solution(mesh):
    in_specs = (
        P(AXES, None, None),
        P(AXES, None, None),
        P(AXES, None, None),
        P(AXES, None),
        P("district", None, None),
        P(AXES),
        P(AXES, None),
    )
    out_specs = (P(AXES, None, None), P(AXES, None, None))
    return jax.shard_map(local, mesh=mesh, in_specs=in_specs, out_specs=out_specs, check_vma=False)
```

```python
import functools

import jax
import jax.numpy as jnp
from jax import lax
from jax.experimental import pallas as pl
from jax.experimental.pallas import tpu as pltpu
from jax.sharding import PartitionSpec as P


SIDE = 4
AXES = ("district", "coarse")
VMEM = pl.BlockSpec(memory_space=pltpu.VMEM)
HBM = pl.BlockSpec(memory_space=pltpu.MemorySpace.HBM)
F32 = jnp.float32
BF16 = jnp.bfloat16
TILE = 8
LANES = 128


def quotient(value, by):
    if by & (by - 1) == 0:
        return lax.shift_right_logical(value, jnp.int32(by.bit_length() - 1))
    return lax.div(value, jnp.int32(by))


def remainder(value, by):
    if by & (by - 1) == 0:
        return lax.bitwise_and(value, jnp.int32(by - 1))
    return lax.rem(value, jnp.int32(by))


def group_of(place, size):
    if size & (size - 1) == 0:
        return lax.shift_right_arithmetic(place, jnp.int32(size.bit_length() - 1))
    return jnp.where(place < 0, -1, lax.div(place, jnp.int32(size)))


def near_side(index):
    return jnp.where(remainder(index, 2) == 0, index + 1, index - 1)


def far_side(index, count):
    return jnp.where(
        remainder(index, 2) == 0,
        jnp.where(index == 0, count - 1, index - 1),
        jnp.where(index == count - 1, 0, index + 1),
    )


def facing(partner_ref, dims):
    index = lax.axis_index("district")
    near = near_side(index)
    far = far_side(index, dims.districts)
    out = []
    for slot in range(dims.slots):
        for block in range(dims.blocks):
            place = partner_ref[slot, block]
            district = group_of(place, dims.coarse * dims.per_device)
            out.append(
                (
                    (district == near).astype(jnp.int32),
                    (district == far).astype(jnp.int32),
                    place,
                )
            )
    return out


def block_of(ref, slot, block):
    return ref[slot, :, block * LANES : (block + 1) * LANES]


def pack_first_kernel(
    dims, partner_hbm, free_hbm, near_ref, far_ref, free_ref, partner_ref, order, sems
):
    fetch_partner = pltpu.make_async_copy(partner_hbm, partner_ref, sems.at[0])
    fetch_free = [
        pltpu.make_async_copy(free_hbm.at[slot], free_ref.at[slot], sems.at[1 + slot])
        for slot in range(dims.slots)
    ]
    fetch_partner.start()
    for fetch in fetch_free:
        fetch.start()
    fetch_partner.wait()
    near_count = jnp.int32(0)
    far_count = jnp.int32(0)
    for place, (near, far, _) in enumerate(facing(partner_ref, dims)):
        slot = jnp.where(near > 0, near_count, jnp.where(far > 0, SIDE + far_count, 2 * SIDE))
        order[slot] = jnp.int32(place)
        near_count += near
        far_count += far
    for fetch in fetch_free:
        fetch.wait()
    for slot in range(2 * SIDE):
        place = order[slot]
        lane = pl.multiple_of(remainder(place, dims.blocks) * LANES, LANES)
        value = free_ref[quotient(place, dims.blocks), :, pl.ds(lane, LANES)]
        if slot < SIDE:
            near_ref[slot] = value
        else:
            far_ref[slot - SIDE] = value


def prepare_kernel(
    dims,
    partner_hbm,
    iface_hbm,
    owner_hbm,
    modes_hbm,
    inverse_hbm,
    flex_hbm,
    others_in,
    take_ref,
    give_ref,
    weight_ref,
    modes_out,
    high_out,
    low_out,
    flex_out,
    partner_ref,
    iface_ref,
    owner_ref,
    modes_ref,
    inverse_ref,
    others_ref,
    partners,
    sems,
):
    pairs = (
        (partner_hbm, partner_ref),
        (iface_hbm, iface_ref),
        (owner_hbm, owner_ref),
        (others_in, others_ref),
        (modes_hbm, modes_ref),
        (inverse_hbm, inverse_ref),
        (flex_hbm, flex_out),
    )
    fetches = [
        pltpu.make_async_copy(there, here, sems.at[i]) for i, (there, here) in enumerate(pairs)
    ]
    for fetch in fetches:
        fetch.start()
    for fetch in fetches[:-1]:
        fetch.wait()
    faces = facing(partner_ref, dims)
    row = lax.broadcasted_iota(jnp.int32, (TILE, LANES), 0)
    near_count = jnp.int32(0)
    far_count = jnp.int32(0)
    for place, (near, far, whole) in enumerate(faces):
        slot = jnp.where(near > 0, near_count, jnp.where(far > 0, SIDE + far_count, 2 * SIDE))
        partners[slot] = remainder(jnp.maximum(whole, 0), dims.per_device)
        give_ref[place] = jnp.where(row == slot, 1.0, 0.0).astype(F32)
        near_count += near
        far_count += far
    for place, (near, far, whole) in enumerate(faces):
        other = remainder(jnp.maximum(whole, 0), dims.per_device)
        slot_id, block_id = divmod(place, dims.blocks)
        from_near = jnp.int32(0)
        from_far = jnp.int32(SIDE)
        for slot in range(SIDE):
            from_near += (partners[slot] < other).astype(jnp.int32)
            from_far += (partners[SIDE + slot] < other).astype(jnp.int32)
        slot = jnp.where(near > 0, from_near, jnp.where(far > 0, from_far, 2 * SIDE))
        take_ref[place] = jnp.where(row == slot, 1.0, 0.0).astype(F32)
        used = (block_id < iface_ref[slot_id]).astype(F32)
        double = used + jnp.maximum(near, far).astype(F32)
        weight_ref[place] = jnp.where(row == 0, used, double)
    member = lax.axis_index("coarse")
    all_slots = dims.slots * dims.coarse
    corner_rows = all_slots * dims.corners
    slot_of_row = quotient(
        lax.broadcasted_iota(jnp.int32, (corner_rows, dims.width), 0), dims.corners
    )
    placed = []
    for slot in range(dims.slots):
        modes = modes_ref[slot].astype(F32)
        stacked = jnp.concatenate([modes] * all_slots, axis=0)
        block = jnp.where(slot_of_row == member * dims.slots + slot, stacked, 0.0).astype(BF16)
        modes_out[:, slot * dims.width : (slot + 1) * dims.width] = block
        placed.append(block)
    corner = lax.broadcasted_iota(jnp.int32, (dims.corners, dims.coarse_width), 0)
    column = lax.broadcasted_iota(jnp.int32, (dims.corners, dims.coarse_width), 1)
    hot, own_hot = [], []
    for place in range(all_slots):
        who, slot = divmod(place, dims.slots)
        owners = jnp.zeros((dims.corners, dims.coarse_width), jnp.int32)
        for k in range(dims.corners):
            if dims.coarse == 2:
                owner = jnp.where(member == who, owner_ref[slot, k], others_ref[slot, k])
            else:
                owner = others_ref[who, slot, k]
            owners = jnp.where(corner == k, owner, owners)
        hot.append(jnp.where(column == owners, 1.0, 0.0).astype(F32))
        own_hot.append(jnp.where(member == who, hot[-1], 0.0))
    onto = jnp.dot(
        jnp.concatenate(hot, axis=0),
        inverse_ref[0],
        precision=lax.Precision.HIGHEST,
        preferred_element_type=F32,
    )
    between = lax.dot_general(
        onto,
        jnp.concatenate(own_hot, axis=0),
        (((1,), (1,)), ((), ())),
        precision=lax.Precision.HIGHEST,
        preferred_element_type=F32,
    )
    pieces = jnp.concatenate(thirds(between), axis=0)
    for slot in range(dims.slots):
        lanes = slice(slot * dims.width, (slot + 1) * dims.width)
        spread = jnp.dot(pieces, placed[slot], preferred_element_type=F32)
        spread = (
            spread[:corner_rows]
            + spread[corner_rows : 2 * corner_rows]
            + spread[2 * corner_rows :]
        )
        high, low = halves(spread)
        high_out[:, lanes] = high
        low_out[:, lanes] = low
    fetches[-1].wait()


def halves(value):
    high = value.astype(BF16)
    low = (value - high.astype(F32)).astype(BF16)
    return high, low


def thirds(value):
    first = value.astype(BF16)
    rest = value - first.astype(F32)
    second, third = halves(rest)
    return first, second, third


def lane_sums(value):
    return jnp.sum(value, axis=0, keepdims=True)


def jump_blocks(dims, field_ref, sides, take_ref, weight_ref):
    for slot in range(dims.slots):
        for block in range(dims.blocks):
            place = slot * dims.blocks + block
            value = block_of(field_ref, slot, block) * weight_ref[place, 0:1, :]
            for side, ref in enumerate(sides):
                for j in range(SIDE):
                    row = side * SIDE + j
                    value = value - take_ref[place, row : row + 1, :] * ref[j]
            yield slot, block, value


def corner_sums(dims, high_parts, low_parts, modes_ref):
    stacked = jnp.concatenate(
        [jnp.concatenate(high_parts, axis=1), jnp.concatenate(low_parts, axis=1)], axis=0
    )
    sums = lax.dot_general(
        stacked, modes_ref[...], (((1,), (1,)), ((), ())), preferred_element_type=F32
    )
    return sums[: dims.scen] + sums[dims.scen :]


def jump_kernel(
    dims,
    field_ref,
    near_ref,
    far_ref,
    take_ref,
    weight_ref,
    modes_ref,
    jump_ref,
    corner_ref,
):
    high_parts, low_parts = [], []
    for slot, block, value in jump_blocks(
        dims, field_ref, (near_ref, far_ref), take_ref, weight_ref
    ):
        jump_ref[slot, :, block * LANES : (block + 1) * LANES] = value
        high, low = halves(value)
        high_parts.append(high)
        low_parts.append(low)
    corner_ref[...] = corner_sums(dims, high_parts, low_parts, modes_ref)


def local_term(dims, direction_ref, flex_ref):
    for slot in range(dims.slots):
        high, low = halves(direction_ref[slot])
        both = jnp.dot(
            jnp.concatenate([high, low], axis=0), flex_ref[slot], preferred_element_type=F32
        )
        yield both[: dims.scen] + both[dims.scen :]


def corner_weights(dims, field_ref, weight_ref, high_ref, low_ref):
    high_parts, low_parts = [], []
    for slot in range(dims.slots):
        for block in range(dims.blocks):
            place = slot * dims.blocks + block
            value = block_of(field_ref, slot, block) * weight_ref[place, 1:2, :]
            high, low = halves(value)
            high_parts.append(high)
            low_parts.append(low)
    high = jnp.concatenate(high_parts, axis=1)
    both = jnp.concatenate([high, jnp.concatenate(low_parts, axis=1)], axis=0)
    contract = (((1,), (1,)), ((), ()))
    part = lax.dot_general(both, high_ref[...], contract, preferred_element_type=F32)
    rest = lax.dot_general(high, low_ref[...], contract, preferred_element_type=F32)
    return part[: dims.scen] + part[dims.scen :] + rest


def local_kernel(dims, direction_ref, flex_ref, weight_ref, high_ref, low_ref, out_ref, g_ref):
    for slot, term in enumerate(local_term(dims, direction_ref, flex_ref)):
        out_ref[slot] = term
    g_ref[...] = corner_weights(dims, direction_ref, weight_ref, high_ref, low_ref)


def local_last_kernel(
    dims,
    direction_ref,
    flex_ref,
    weight_ref,
    high_ref,
    low_ref,
    rhs_ref,
    out_ref,
    g_ref,
    sums_ref,
):
    acc = [jnp.zeros((dims.scen, LANES), F32)] * 5
    for slot, term in enumerate(local_term(dims, direction_ref, flex_ref)):
        out_ref[slot] = term
        for block in range(dims.blocks):
            rhs = block_of(rhs_ref, slot, block)
            image = block_of(direction_ref, slot, block)
            doubled = (
                weight_ref[slot * dims.blocks + block, 1:2, :]
                * term[:, block * LANES : (block + 1) * LANES]
            )
            for q, product in enumerate(
                (rhs * rhs, rhs * image, image * image, rhs * doubled, image * doubled)
            ):
                acc[q] = acc[q] + product
    sums_ref[...] = totals_of(rows_of(acc, 0))
    g_ref[...] = corner_weights(dims, direction_ref, weight_ref, high_ref, low_ref)


def totals_of(tile):
    totals = jnp.sum(tile, axis=1, keepdims=True)
    return lane_sums(jnp.where(on_diagonal(), totals, 0.0))


def rows_of(parts, first):
    lanes = parts[0].shape[1]
    row = lax.broadcasted_iota(jnp.int32, (TILE, lanes), 0)
    tile = jnp.zeros((TILE, lanes), F32)
    for q, part in enumerate(parts):
        tile = jnp.where(row == first + q, lane_sums(part), tile)
    return tile


def on_diagonal():
    row = lax.broadcasted_iota(jnp.int32, (TILE, LANES), 0)
    return row == lax.broadcasted_iota(jnp.int32, (TILE, LANES), 1)


def add_coarse(dims, local_ref, sums, high_ref, low_ref):
    high, low = halves(sums)
    both = jnp.concatenate([high, low], axis=0)
    for slot in range(dims.slots):
        lanes = slice(slot * dims.width, (slot + 1) * dims.width)
        part = jnp.dot(both, high_ref[:, lanes], preferred_element_type=F32)
        rest = jnp.dot(high, low_ref[:, lanes], preferred_element_type=F32)
        yield local_ref[slot] + (part[: dims.scen] + part[dims.scen :] + rest)


def pack(dims, response, give_ref, near_ref, far_ref):
    for side, ref in enumerate((near_ref, far_ref)):
        for j in range(SIDE):
            row = side * SIDE + j
            value = jnp.zeros((dims.scen, LANES), F32)
            for place in range(dims.per_device):
                slot, block = divmod(place, dims.blocks)
                part = response[slot][:, block * LANES : (block + 1) * LANES]
                value = value + give_ref[place, row : row + 1, :] * part
            ref[j] = value


def respond_kernel(
    dims,
    local_ref,
    own_ref,
    other_ref,
    high_ref,
    low_ref,
    give_ref,
    out_ref,
    near_ref,
    far_ref,
):
    response = list(add_coarse(dims, local_ref, own_ref[...] + other_ref[...], high_ref, low_ref))
    for slot in range(dims.slots):
        out_ref[slot] = response[slot]
    pack(dims, response, give_ref, near_ref, far_ref)


def respond_last_kernel(
    dims,
    local_ref,
    own_ref,
    other_ref,
    high_ref,
    low_ref,
    give_ref,
    rhs_g_ref,
    image_g_ref,
    early_ref,
    out_ref,
    near_ref,
    far_ref,
    sums_hbm,
    sums_ref,
    sem,
):
    corner = own_ref[...] + other_ref[...]
    late = totals_of(rows_of((corner * rhs_g_ref[...], corner * image_g_ref[...]), 3))
    sums_ref[...] = jnp.broadcast_to((early_ref[...] + late)[None], sums_ref.shape)
    put = pltpu.make_async_copy(sums_ref, sums_hbm, sem)
    put.start()
    response = list(add_coarse(dims, local_ref, corner, high_ref, low_ref))
    for slot in range(dims.slots):
        out_ref[slot] = response[slot]
    pack(dims, response, give_ref, near_ref, far_ref)
    put.wait()


def settle_kernel(
    dims,
    sums_ref,
    rhs_ref,
    image_ref,
    field_ref,
    near_ref,
    take_ref,
    weight_ref,
    multiplier_ref,
    residual_ref,
    factor_ref,
):
    row = lane_sums(sums_ref[...])
    totals = jnp.sum(jnp.where(on_diagonal(), row, 0.0), axis=1, keepdims=True)
    norm, first, square, cross, second = (totals[q : q + 1, :] for q in range(5))
    step = norm / first
    norm_next = norm - 2.0 * step * first + step * step * square
    grown = 1.0 + norm_next / norm
    curve = grown * grown * first - grown * step * (cross + square) + step * step * second
    step_next = norm_next / curve
    on_first = step + step_next * grown
    on_second = step_next * step
    factor_ref[...] = jnp.broadcast_to(on_second, factor_ref.shape)
    for slot, block, second_image in jump_blocks(
        dims, field_ref, (near_ref,), take_ref, weight_ref
    ):
        lanes = slice(block * LANES, (block + 1) * LANES)
        rhs = rhs_ref[slot, :, lanes]
        image = image_ref[slot, :, lanes]
        multiplier_ref[slot, :, lanes] = on_first * rhs - on_second * image
        residual_ref[slot, :, lanes] = rhs - on_first * image + on_second * second_image


def finish_kernel(
    dims,
    multiplier_ref,
    partial_ref,
    factor_ref,
    far_ref,
    take_ref,
    multiplier_hbm,
    residual_hbm,
    residual_ref,
    sems,
):
    puts = [
        pltpu.make_async_copy(
            multiplier_ref.at[slot], multiplier_hbm.at[slot], sems.at[0, slot]
        )
        for slot in range(dims.slots)
    ]
    for put in puts:
        put.start()
    factor = factor_ref[0:1, :]
    sides = [factor * far_ref[j] for j in range(SIDE)]
    for slot in range(dims.slots):
        for block in range(dims.blocks):
            place = slot * dims.blocks + block
            lanes = slice(block * LANES, (block + 1) * LANES)
            value = partial_ref[slot, :, lanes]
            for j in range(SIDE):
                value = value - take_ref[place, SIDE + j : SIDE + j + 1, :] * sides[j]
            residual_ref[slot, :, lanes] = value
        put = pltpu.make_async_copy(residual_ref.at[slot], residual_hbm.at[slot], sems.at[1, slot])
        put.start()
        puts.append(put)
    for put in puts:
        put.wait()


class Dims:
    pass


def stay(value):
    return pltpu.with_memory_space_constraint(value, pltpu.MemorySpace.HBM)


def call(kernel, dims, outs, args, in_specs=None, out_specs=None, scratch=(), cost=None):
    return pl.pallas_call(
        functools.partial(kernel, dims),
        out_shape=outs,
        in_specs=in_specs if in_specs is not None else [VMEM] * len(args),
        out_specs=out_specs if out_specs is not None else jax.tree.map(lambda _: VMEM, outs),
        scratch_shapes=list(scratch),
        compiler_params=pltpu.CompilerParams(vmem_limit_bytes=16 << 20),
        cost_estimate=cost,
    )(*args)


def local(
    free_response, flexibility, corner_modes, corner_owner, coarse_inverse, iface_blocks, partner
):
    dims = Dims()
    dims.slots, dims.scen, dims.width = free_response.shape
    dims.blocks = partner.shape[1]
    dims.per_device = dims.slots * dims.blocks
    dims.coarse_width = coarse_inverse.shape[1]
    dims.corners = corner_modes.shape[1]
    dims.districts = lax.axis_size("district")
    dims.coarse = lax.axis_size("coarse")
    devices = dims.districts * dims.coarse
    shape = jax.ShapeDtypeStruct
    whole = shape(free_response.shape, F32)
    packed = shape((SIDE, dims.scen, LANES), F32)
    per_block = shape((dims.per_device, TILE, LANES), F32)
    corner_rows = dims.slots * dims.corners * dims.coarse

    near_pairs = [(d, d + 1 if d % 2 == 0 else d - 1) for d in range(dims.districts)]
    far_pairs = [
        (d, (d - 1 if d % 2 == 0 else d + 1) % dims.districts) for d in range(dims.districts)
    ]

    def exchange(near, far):
        far = lax.ppermute(far, "district", far_pairs)
        near = lax.ppermute(near, "district", near_pairs)
        return near, far

    def from_group(value):
        if dims.coarse == 2:
            return lax.ppermute(value, "coarse", [(0, 1), (1, 0)])
        return lax.psum(value, "coarse") - value

    near, far, field = call(
        pack_first_kernel,
        dims,
        (packed, packed, whole),
        (stay(partner), stay(free_response)),
        in_specs=[HBM, HBM],
        scratch=[
            pltpu.SMEM(partner.shape, jnp.int32),
            pltpu.SMEM((2 * SIDE + 1,), jnp.int32),
            pltpu.SemaphoreType.DMA((1 + dims.slots,)),
        ],
    )
    near, far = exchange(near, far)
    if dims.coarse == 2:
        others = lax.ppermute(corner_owner, "coarse", [(0, 1), (1, 0)])
    else:
        others = lax.all_gather(corner_owner, "coarse")
    take, give, weight, modes, high, low, flex = call(
        prepare_kernel,
        dims,
        (
            per_block,
            per_block,
            per_block,
            shape((corner_rows, dims.slots * dims.width), BF16),
            shape((corner_rows, dims.slots * dims.width), BF16),
            shape((corner_rows, dims.slots * dims.width), BF16),
            shape(flexibility.shape, BF16),
        ),
        tuple(
            stay(value)
            for value in (
                partner,
                iface_blocks,
                corner_owner,
                corner_modes,
                coarse_inverse,
                flexibility,
            )
        )
        + (others,),
        in_specs=[HBM] * 6 + [VMEM],
        scratch=[
            pltpu.SMEM(partner.shape, jnp.int32),
            pltpu.SMEM(iface_blocks.shape, jnp.int32),
            pltpu.SMEM(corner_owner.shape, jnp.int32),
            pltpu.VMEM(corner_modes.shape, BF16),
            pltpu.VMEM(coarse_inverse.shape, F32),
            pltpu.SMEM(others.shape, jnp.int32),
            pltpu.SMEM((2 * SIDE + 1,), jnp.int32),
            pltpu.SemaphoreType.DMA((7,)),
        ],
        cost=pl.CostEstimate(flops=10**7, bytes_accessed=4 * 10**6, transcendentals=0),
    )

    def jump(field, near, far):
        return call(
            jump_kernel,
            dims,
            (whole, shape((dims.scen, corner_rows), F32)),
            (field, near, far, take, weight, modes),
        )

    matmul_cost = pl.CostEstimate(flops=10**8, bytes_accessed=3 * 10**6, transcendentals=0)
    rhs, part = jump(field, near, far)
    other = from_group(part)
    corners = shape((dims.scen, corner_rows), F32)
    term, rhs_g = call(
        local_kernel,
        dims,
        (whole, corners),
        (rhs, flex, weight, high, low),
        cost=matmul_cost,
    )
    response, near, far = call(
        respond_kernel,
        dims,
        (whole, packed, packed),
        (term, part, other, high, low, give),
    )
    near, far = exchange(near, far)
    image, part = jump(response, near, far)
    other = from_group(part)
    term, image_g, early = call(
        local_last_kernel,
        dims,
        (whole, corners, shape((1, LANES), F32)),
        (image, flex, weight, high, low, rhs),
        cost=matmul_cost,
    )
    response, near, far, sums = call(
        respond_last_kernel,
        dims,
        (whole, packed, packed, shape((devices, 1, LANES), F32)),
        (term, part, other, high, low, give, rhs_g, image_g, early),
        out_specs=(VMEM, VMEM, VMEM, HBM),
        scratch=[pltpu.VMEM((devices, 1, LANES), F32), pltpu.SemaphoreType.DMA],
    )
    sums = lax.all_to_all(sums, AXES, 0, 0)
    near, far = exchange(near, far)
    multiplier, residual, factor = call(
        settle_kernel,
        dims,
        (whole, whole, shape((TILE, LANES), F32)),
        (sums.reshape(devices, LANES), rhs, image, response, near, take, weight),
    )
    return call(
        finish_kernel,
        dims,
        (whole, whole),
        (multiplier, residual, factor, far, take),
        out_specs=(HBM, HBM),
        scratch=[pltpu.VMEM(free_response.shape, F32), pltpu.SemaphoreType.DMA((2, dims.slots))],
    )


def solution(mesh):
    in_specs = (
        P(AXES, None, None),
        P(AXES, None, None),
        P(AXES, None, None),
        P(AXES, None),
        P("district", None, None),
        P(AXES),
        P(AXES, None),
    )
    out_specs = (P(AXES, None, None), P(AXES, None, None))
    return jax.shard_map(local, mesh=mesh, in_specs=in_specs, out_specs=out_specs, check_vma=False)
```

```python
import functools

import jax
import jax.numpy as jnp
from jax import lax
from jax.experimental import pallas as pl
from jax.experimental.pallas import tpu as pltpu
from jax.sharding import PartitionSpec as P


SIDE = 4
AXES = ("district", "coarse")
VMEM = pl.BlockSpec(memory_space=pltpu.VMEM)
HBM = pl.BlockSpec(memory_space=pltpu.MemorySpace.HBM)
F32 = jnp.float32
BF16 = jnp.bfloat16
TILE = 8
LANES = 128


def quotient(value, by):
    if by & (by - 1) == 0:
        return lax.shift_right_logical(value, jnp.int32(by.bit_length() - 1))
    return lax.div(value, jnp.int32(by))


def remainder(value, by):
    if by & (by - 1) == 0:
        return lax.bitwise_and(value, jnp.int32(by - 1))
    return lax.rem(value, jnp.int32(by))


def group_of(place, size):
    if size & (size - 1) == 0:
        return lax.shift_right_arithmetic(place, jnp.int32(size.bit_length() - 1))
    return jnp.where(place < 0, -1, lax.div(place, jnp.int32(size)))


def near_side(index):
    return jnp.where(remainder(index, 2) == 0, index + 1, index - 1)


def far_side(index, count):
    return jnp.where(
        remainder(index, 2) == 0,
        jnp.where(index == 0, count - 1, index - 1),
        jnp.where(index == count - 1, 0, index + 1),
    )


def facing(partner_ref, dims):
    index = lax.axis_index("district")
    near = near_side(index)
    far = far_side(index, dims.districts)
    out = []
    for slot in range(dims.slots):
        for block in range(dims.blocks):
            place = partner_ref[slot, block]
            district = group_of(place, dims.coarse * dims.per_device)
            out.append(
                (
                    (district == near).astype(jnp.int32),
                    (district == far).astype(jnp.int32),
                    place,
                )
            )
    return out


def block_of(ref, slot, block):
    return ref[slot, :, block * LANES : (block + 1) * LANES]


def pack_first_kernel(
    dims, partner_hbm, free_hbm, near_ref, far_ref, free_ref, partner_ref, order, sems
):
    fetch_partner = pltpu.make_async_copy(partner_hbm, partner_ref, sems.at[0])
    fetch_free = [
        pltpu.make_async_copy(free_hbm.at[slot], free_ref.at[slot], sems.at[1 + slot])
        for slot in range(dims.slots)
    ]
    fetch_partner.start()
    for fetch in fetch_free:
        fetch.start()
    fetch_partner.wait()
    near_count = jnp.int32(0)
    far_count = jnp.int32(0)
    for place, (near, far, _) in enumerate(facing(partner_ref, dims)):
        slot = jnp.where(near > 0, near_count, jnp.where(far > 0, SIDE + far_count, 2 * SIDE))
        order[slot] = jnp.int32(place)
        near_count += near
        far_count += far
    for fetch in fetch_free:
        fetch.wait()
    for slot in range(2 * SIDE):
        place = order[slot]
        lane = pl.multiple_of(remainder(place, dims.blocks) * LANES, LANES)
        value = free_ref[quotient(place, dims.blocks), :, pl.ds(lane, LANES)]
        if slot < SIDE:
            near_ref[slot] = value
        else:
            far_ref[slot - SIDE] = value


def prepare_kernel(
    dims,
    partner_hbm,
    iface_hbm,
    owner_hbm,
    modes_hbm,
    inverse_hbm,
    flex_hbm,
    others_in,
    take_ref,
    give_ref,
    weight_ref,
    modes_out,
    high_out,
    low_out,
    flex_out,
    partner_ref,
    iface_ref,
    owner_ref,
    modes_ref,
    inverse_ref,
    others_ref,
    partners,
    sems,
):
    pairs = (
        (partner_hbm, partner_ref),
        (iface_hbm, iface_ref),
        (owner_hbm, owner_ref),
        (others_in, others_ref),
        (modes_hbm, modes_ref),
        (inverse_hbm, inverse_ref),
        (flex_hbm, flex_out),
    )
    fetches = [
        pltpu.make_async_copy(there, here, sems.at[i]) for i, (there, here) in enumerate(pairs)
    ]
    for fetch in fetches:
        fetch.start()
    for fetch in fetches[:-1]:
        fetch.wait()
    faces = facing(partner_ref, dims)
    row = lax.broadcasted_iota(jnp.int32, (TILE, LANES), 0)
    near_count = jnp.int32(0)
    far_count = jnp.int32(0)
    for place, (near, far, whole) in enumerate(faces):
        slot = jnp.where(near > 0, near_count, jnp.where(far > 0, SIDE + far_count, 2 * SIDE))
        partners[slot] = remainder(jnp.maximum(whole, 0), dims.per_device)
        give_ref[place] = jnp.where(row == slot, 1.0, 0.0).astype(F32)
        near_count += near
        far_count += far
    for place, (near, far, whole) in enumerate(faces):
        other = remainder(jnp.maximum(whole, 0), dims.per_device)
        slot_id, block_id = divmod(place, dims.blocks)
        from_near = jnp.int32(0)
        from_far = jnp.int32(SIDE)
        for slot in range(SIDE):
            from_near += (partners[slot] < other).astype(jnp.int32)
            from_far += (partners[SIDE + slot] < other).astype(jnp.int32)
        slot = jnp.where(near > 0, from_near, jnp.where(far > 0, from_far, 2 * SIDE))
        take_ref[place] = jnp.where(row == slot, 1.0, 0.0).astype(F32)
        used = (block_id < iface_ref[slot_id]).astype(F32)
        double = used + jnp.maximum(near, far).astype(F32)
        weight_ref[place] = jnp.where(row == 0, used, double)
    member = lax.axis_index("coarse")
    all_slots = dims.slots * dims.coarse
    corner_rows = all_slots * dims.corners
    slot_of_row = quotient(
        lax.broadcasted_iota(jnp.int32, (corner_rows, dims.width), 0), dims.corners
    )
    placed = []
    for slot in range(dims.slots):
        modes = modes_ref[slot].astype(F32)
        stacked = jnp.concatenate([modes] * all_slots, axis=0)
        block = jnp.where(slot_of_row == member * dims.slots + slot, stacked, 0.0).astype(BF16)
        modes_out[:, slot * dims.width : (slot + 1) * dims.width] = block
        placed.append(block)
    corner = lax.broadcasted_iota(jnp.int32, (dims.corners, dims.coarse_width), 0)
    column = lax.broadcasted_iota(jnp.int32, (dims.corners, dims.coarse_width), 1)
    hot, own_hot = [], []
    for place in range(all_slots):
        who, slot = divmod(place, dims.slots)
        owners = jnp.zeros((dims.corners, dims.coarse_width), jnp.int32)
        for k in range(dims.corners):
            if dims.coarse == 2:
                owner = jnp.where(member == who, owner_ref[slot, k], others_ref[slot, k])
            else:
                owner = others_ref[who, slot, k]
            owners = jnp.where(corner == k, owner, owners)
        hot.append(jnp.where(column == owners, 1.0, 0.0).astype(F32))
        own_hot.append(jnp.where(member == who, hot[-1], 0.0))
    onto = jnp.dot(
        jnp.concatenate(hot, axis=0),
        inverse_ref[0],
        precision=lax.Precision.HIGHEST,
        preferred_element_type=F32,
    )
    between = lax.dot_general(
        onto,
        jnp.concatenate(own_hot, axis=0),
        (((1,), (1,)), ((), ())),
        precision=lax.Precision.HIGHEST,
        preferred_element_type=F32,
    )
    pieces = jnp.concatenate(thirds(between), axis=0)
    for slot in range(dims.slots):
        lanes = slice(slot * dims.width, (slot + 1) * dims.width)
        spread = jnp.dot(pieces, placed[slot], preferred_element_type=F32)
        spread = (
            spread[:corner_rows]
            + spread[corner_rows : 2 * corner_rows]
            + spread[2 * corner_rows :]
        )
        high, low = halves(spread)
        high_out[:, lanes] = high
        low_out[:, lanes] = low
    fetches[-1].wait()


def halves(value):
    high = value.astype(BF16)
    low = (value - high.astype(F32)).astype(BF16)
    return high, low


def thirds(value):
    first = value.astype(BF16)
    rest = value - first.astype(F32)
    second, third = halves(rest)
    return first, second, third


def lane_sums(value):
    return jnp.sum(value, axis=0, keepdims=True)


def jump_blocks(dims, field_ref, sides, take_ref, weight_ref):
    for slot in range(dims.slots):
        for block in range(dims.blocks):
            place = slot * dims.blocks + block
            value = block_of(field_ref, slot, block) * weight_ref[place, 0:1, :]
            for side, ref in enumerate(sides):
                for j in range(SIDE):
                    row = side * SIDE + j
                    value = value - take_ref[place, row : row + 1, :] * ref[j]
            yield slot, block, value


def corner_sums(dims, parts, modes_ref):
    stacked = jnp.concatenate([jnp.concatenate(part, axis=1) for part in parts], axis=0)
    sums = lax.dot_general(
        stacked, modes_ref[...], (((1,), (1,)), ((), ())), preferred_element_type=F32
    )
    return folded(dims, sums)


def folded(dims, rows):
    groups = [rows[i : i + dims.scen] for i in range(0, rows.shape[0], dims.scen)]
    return functools.reduce(jnp.add, groups)


def jump_kernel(
    dims,
    field_ref,
    near_ref,
    far_ref,
    take_ref,
    weight_ref,
    modes_ref,
    jump_ref,
    corner_ref,
    pieces,
):
    parts = [[] for _ in range(pieces)]
    for slot, block, value in jump_blocks(
        dims, field_ref, (near_ref, far_ref), take_ref, weight_ref
    ):
        jump_ref[slot, :, block * LANES : (block + 1) * LANES] = value
        for part, piece in zip(parts, halves(value)):
            part.append(piece)
    corner_ref[...] = corner_sums(dims, parts, modes_ref)


def local_term(dims, pieces, direction_ref, flex_ref):
    for slot in range(dims.slots):
        forces = jnp.concatenate(halves(direction_ref[slot])[:pieces], axis=0)
        yield folded(dims, jnp.dot(forces, flex_ref[slot], preferred_element_type=F32))


def corner_weights(dims, field_ref, weight_ref, high_ref, low_ref):
    high_parts, low_parts = [], []
    for slot in range(dims.slots):
        for block in range(dims.blocks):
            place = slot * dims.blocks + block
            value = block_of(field_ref, slot, block) * weight_ref[place, 1:2, :]
            high, low = halves(value)
            high_parts.append(high)
            low_parts.append(low)
    high = jnp.concatenate(high_parts, axis=1)
    both = jnp.concatenate([high, jnp.concatenate(low_parts, axis=1)], axis=0)
    contract = (((1,), (1,)), ((), ()))
    part = lax.dot_general(both, high_ref[...], contract, preferred_element_type=F32)
    rest = lax.dot_general(high, low_ref[...], contract, preferred_element_type=F32)
    return part[: dims.scen] + part[dims.scen :] + rest


def local_kernel(dims, direction_ref, flex_ref, weight_ref, high_ref, low_ref, out_ref, g_ref):
    for slot, term in enumerate(local_term(dims, 1, direction_ref, flex_ref)):
        out_ref[slot] = term
    g_ref[...] = corner_weights(dims, direction_ref, weight_ref, high_ref, low_ref)


def local_last_kernel(
    dims,
    direction_ref,
    flex_ref,
    weight_ref,
    high_ref,
    low_ref,
    rhs_ref,
    out_ref,
    g_ref,
    sums_ref,
):
    acc = [jnp.zeros((dims.scen, LANES), F32)] * 5
    for slot, term in enumerate(local_term(dims, 2, direction_ref, flex_ref)):
        out_ref[slot] = term
        for block in range(dims.blocks):
            rhs = block_of(rhs_ref, slot, block)
            image = block_of(direction_ref, slot, block)
            doubled = (
                weight_ref[slot * dims.blocks + block, 1:2, :]
                * term[:, block * LANES : (block + 1) * LANES]
            )
            for q, product in enumerate(
                (rhs * rhs, rhs * image, image * image, rhs * doubled, image * doubled)
            ):
                acc[q] = acc[q] + product
    sums_ref[...] = totals_of(rows_of(acc, 0))
    g_ref[...] = corner_weights(dims, direction_ref, weight_ref, high_ref, low_ref)


def totals_of(tile):
    totals = jnp.sum(tile, axis=1, keepdims=True)
    return lane_sums(jnp.where(on_diagonal(), totals, 0.0))


def rows_of(parts, first):
    lanes = parts[0].shape[1]
    row = lax.broadcasted_iota(jnp.int32, (TILE, lanes), 0)
    tile = jnp.zeros((TILE, lanes), F32)
    for q, part in enumerate(parts):
        tile = jnp.where(row == first + q, lane_sums(part), tile)
    return tile


def on_diagonal():
    row = lax.broadcasted_iota(jnp.int32, (TILE, LANES), 0)
    return row == lax.broadcasted_iota(jnp.int32, (TILE, LANES), 1)


def add_coarse(dims, local_ref, sums, high_ref, low_ref):
    high, low = halves(sums)
    both = jnp.concatenate([high, low], axis=0)
    for slot in range(dims.slots):
        lanes = slice(slot * dims.width, (slot + 1) * dims.width)
        part = jnp.dot(both, high_ref[:, lanes], preferred_element_type=F32)
        rest = jnp.dot(high, low_ref[:, lanes], preferred_element_type=F32)
        yield local_ref[slot] + (part[: dims.scen] + part[dims.scen :] + rest)


def pack(dims, response, give_ref, near_ref, far_ref):
    for side, ref in enumerate((near_ref, far_ref)):
        for j in range(SIDE):
            row = side * SIDE + j
            value = jnp.zeros((dims.scen, LANES), F32)
            for place in range(dims.per_device):
                slot, block = divmod(place, dims.blocks)
                part = response[slot][:, block * LANES : (block + 1) * LANES]
                value = value + give_ref[place, row : row + 1, :] * part
            ref[j] = value


def respond_kernel(
    dims,
    local_ref,
    own_ref,
    other_ref,
    high_ref,
    low_ref,
    give_ref,
    out_ref,
    near_ref,
    far_ref,
):
    response = list(add_coarse(dims, local_ref, own_ref[...] + other_ref[...], high_ref, low_ref))
    for slot in range(dims.slots):
        out_ref[slot] = response[slot]
    pack(dims, response, give_ref, near_ref, far_ref)


def respond_last_kernel(
    dims,
    local_ref,
    own_ref,
    other_ref,
    high_ref,
    low_ref,
    give_ref,
    rhs_g_ref,
    image_g_ref,
    early_ref,
    out_ref,
    near_ref,
    far_ref,
    sums_hbm,
    sums_ref,
    sem,
):
    corner = own_ref[...] + other_ref[...]
    late = totals_of(rows_of((corner * rhs_g_ref[...], corner * image_g_ref[...]), 3))
    sums_ref[...] = jnp.broadcast_to((early_ref[...] + late)[None], sums_ref.shape)
    put = pltpu.make_async_copy(sums_ref, sums_hbm, sem)
    put.start()
    response = list(add_coarse(dims, local_ref, corner, high_ref, low_ref))
    for slot in range(dims.slots):
        out_ref[slot] = response[slot]
    pack(dims, response, give_ref, near_ref, far_ref)
    put.wait()


def settle_kernel(
    dims,
    sums_ref,
    rhs_ref,
    image_ref,
    field_ref,
    near_ref,
    take_ref,
    weight_ref,
    multiplier_ref,
    residual_ref,
    factor_ref,
):
    row = lane_sums(sums_ref[...])
    totals = jnp.sum(jnp.where(on_diagonal(), row, 0.0), axis=1, keepdims=True)
    norm, first, square, cross, second = (totals[q : q + 1, :] for q in range(5))
    step = norm / first
    norm_next = norm - 2.0 * step * first + step * step * square
    grown = 1.0 + norm_next / norm
    curve = grown * grown * first - grown * step * (cross + square) + step * step * second
    step_next = norm_next / curve
    on_first = step + step_next * grown
    on_second = step_next * step
    factor_ref[...] = jnp.broadcast_to(on_second, factor_ref.shape)
    for slot, block, second_image in jump_blocks(
        dims, field_ref, (near_ref,), take_ref, weight_ref
    ):
        lanes = slice(block * LANES, (block + 1) * LANES)
        rhs = rhs_ref[slot, :, lanes]
        image = image_ref[slot, :, lanes]
        multiplier_ref[slot, :, lanes] = on_first * rhs - on_second * image
        residual_ref[slot, :, lanes] = rhs - on_first * image + on_second * second_image


def finish_kernel(
    dims,
    multiplier_ref,
    partial_ref,
    factor_ref,
    far_ref,
    take_ref,
    multiplier_hbm,
    residual_hbm,
    residual_ref,
    sems,
):
    puts = [
        pltpu.make_async_copy(
            multiplier_ref.at[slot], multiplier_hbm.at[slot], sems.at[0, slot]
        )
        for slot in range(dims.slots)
    ]
    for put in puts:
        put.start()
    factor = factor_ref[0:1, :]
    sides = [factor * far_ref[j] for j in range(SIDE)]
    for slot in range(dims.slots):
        for block in range(dims.blocks):
            place = slot * dims.blocks + block
            lanes = slice(block * LANES, (block + 1) * LANES)
            value = partial_ref[slot, :, lanes]
            for j in range(SIDE):
                value = value - take_ref[place, SIDE + j : SIDE + j + 1, :] * sides[j]
            residual_ref[slot, :, lanes] = value
        put = pltpu.make_async_copy(residual_ref.at[slot], residual_hbm.at[slot], sems.at[1, slot])
        put.start()
        puts.append(put)
    for put in puts:
        put.wait()


class Dims:
    pass


def stay(value):
    return pltpu.with_memory_space_constraint(value, pltpu.MemorySpace.HBM)


def call(kernel, dims, outs, args, in_specs=None, out_specs=None, scratch=(), cost=None):
    return pl.pallas_call(
        functools.partial(kernel, dims),
        out_shape=outs,
        in_specs=in_specs if in_specs is not None else [VMEM] * len(args),
        out_specs=out_specs if out_specs is not None else jax.tree.map(lambda _: VMEM, outs),
        scratch_shapes=list(scratch),
        compiler_params=pltpu.CompilerParams(vmem_limit_bytes=16 << 20),
        cost_estimate=cost,
    )(*args)


def local(
    free_response, flexibility, corner_modes, corner_owner, coarse_inverse, iface_blocks, partner
):
    dims = Dims()
    dims.slots, dims.scen, dims.width = free_response.shape
    dims.blocks = partner.shape[1]
    dims.per_device = dims.slots * dims.blocks
    dims.coarse_width = coarse_inverse.shape[1]
    dims.corners = corner_modes.shape[1]
    dims.districts = lax.axis_size("district")
    dims.coarse = lax.axis_size("coarse")
    devices = dims.districts * dims.coarse
    shape = jax.ShapeDtypeStruct
    whole = shape(free_response.shape, F32)
    packed = shape((SIDE, dims.scen, LANES), F32)
    per_block = shape((dims.per_device, TILE, LANES), F32)
    corner_rows = dims.slots * dims.corners * dims.coarse

    near_pairs = [(d, d + 1 if d % 2 == 0 else d - 1) for d in range(dims.districts)]
    far_pairs = [
        (d, (d - 1 if d % 2 == 0 else d + 1) % dims.districts) for d in range(dims.districts)
    ]

    def exchange(near, far):
        far = lax.ppermute(far, "district", far_pairs)
        near = lax.ppermute(near, "district", near_pairs)
        return near, far

    def from_group(value):
        if dims.coarse == 2:
            return lax.ppermute(value, "coarse", [(0, 1), (1, 0)])
        return lax.psum(value, "coarse") - value

    near, far, field = call(
        pack_first_kernel,
        dims,
        (packed, packed, whole),
        (stay(partner), stay(free_response)),
        in_specs=[HBM, HBM],
        scratch=[
            pltpu.SMEM(partner.shape, jnp.int32),
            pltpu.SMEM((2 * SIDE + 1,), jnp.int32),
            pltpu.SemaphoreType.DMA((1 + dims.slots,)),
        ],
    )
    near, far = exchange(near, far)
    if dims.coarse == 2:
        others = lax.ppermute(corner_owner, "coarse", [(0, 1), (1, 0)])
    else:
        others = lax.all_gather(corner_owner, "coarse")
    take, give, weight, modes, high, low, flex = call(
        prepare_kernel,
        dims,
        (
            per_block,
            per_block,
            per_block,
            shape((corner_rows, dims.slots * dims.width), BF16),
            shape((corner_rows, dims.slots * dims.width), BF16),
            shape((corner_rows, dims.slots * dims.width), BF16),
            shape(flexibility.shape, BF16),
        ),
        tuple(
            stay(value)
            for value in (
                partner,
                iface_blocks,
                corner_owner,
                corner_modes,
                coarse_inverse,
                flexibility,
            )
        )
        + (others,),
        in_specs=[HBM] * 6 + [VMEM],
        scratch=[
            pltpu.SMEM(partner.shape, jnp.int32),
            pltpu.SMEM(iface_blocks.shape, jnp.int32),
            pltpu.SMEM(corner_owner.shape, jnp.int32),
            pltpu.VMEM(corner_modes.shape, BF16),
            pltpu.VMEM(coarse_inverse.shape, F32),
            pltpu.SMEM(others.shape, jnp.int32),
            pltpu.SMEM((2 * SIDE + 1,), jnp.int32),
            pltpu.SemaphoreType.DMA((7,)),
        ],
        cost=pl.CostEstimate(flops=10**7, bytes_accessed=4 * 10**6, transcendentals=0),
    )

    def jump(field, near, far, pieces):
        return call(
            functools.partial(jump_kernel, pieces=pieces),
            dims,
            (whole, shape((dims.scen, corner_rows), F32)),
            (field, near, far, take, weight, modes),
        )

    matmul_cost = pl.CostEstimate(flops=10**8, bytes_accessed=3 * 10**6, transcendentals=0)
    rhs, part = jump(field, near, far, 1)
    other = from_group(part)
    corners = shape((dims.scen, corner_rows), F32)
    term, rhs_g = call(
        local_kernel,
        dims,
        (whole, corners),
        (rhs, flex, weight, high, low),
        cost=matmul_cost,
    )
    response, near, far = call(
        respond_kernel,
        dims,
        (whole, packed, packed),
        (term, part, other, high, low, give),
    )
    near, far = exchange(near, far)
    image, part = jump(response, near, far, 2)
    other = from_group(part)
    term, image_g, early = call(
        local_last_kernel,
        dims,
        (whole, corners, shape((1, LANES), F32)),
        (image, flex, weight, high, low, rhs),
        cost=matmul_cost,
    )
    response, near, far, sums = call(
        respond_last_kernel,
        dims,
        (whole, packed, packed, shape((devices, 1, LANES), F32)),
        (term, part, other, high, low, give, rhs_g, image_g, early),
        out_specs=(VMEM, VMEM, VMEM, HBM),
        scratch=[pltpu.VMEM((devices, 1, LANES), F32), pltpu.SemaphoreType.DMA],
    )
    sums = lax.all_to_all(sums, AXES, 0, 0)
    near, far = exchange(near, far)
    multiplier, residual, factor = call(
        settle_kernel,
        dims,
        (whole, whole, shape((TILE, LANES), F32)),
        (sums.reshape(devices, LANES), rhs, image, response, near, take, weight),
    )
    return call(
        finish_kernel,
        dims,
        (whole, whole),
        (multiplier, residual, factor, far, take),
        out_specs=(HBM, HBM),
        scratch=[pltpu.VMEM(free_response.shape, F32), pltpu.SemaphoreType.DMA((2, dims.slots))],
    )


def solution(mesh):
    in_specs = (
        P(AXES, None, None),
        P(AXES, None, None),
        P(AXES, None, None),
        P(AXES, None),
        P("district", None, None),
        P(AXES),
        P(AXES, None),
    )
    out_specs = (P(AXES, None, None), P(AXES, None, None))
    return jax.shard_map(local, mesh=mesh, in_specs=in_specs, out_specs=out_specs, check_vma=False)
```

```python
import functools

import jax
import jax.numpy as jnp
from jax import lax
from jax.experimental import pallas as pl
from jax.experimental.pallas import tpu as pltpu
from jax.sharding import PartitionSpec as P


SIDE = 4
AXES = ("district", "coarse")
VMEM = pl.BlockSpec(memory_space=pltpu.VMEM)
HBM = pl.BlockSpec(memory_space=pltpu.MemorySpace.HBM)
F32 = jnp.float32
BF16 = jnp.bfloat16
TILE = 8
LANES = 128


def quotient(value, by):
    if by & (by - 1) == 0:
        return lax.shift_right_logical(value, jnp.int32(by.bit_length() - 1))
    return lax.div(value, jnp.int32(by))


def remainder(value, by):
    if by & (by - 1) == 0:
        return lax.bitwise_and(value, jnp.int32(by - 1))
    return lax.rem(value, jnp.int32(by))


def group_of(place, size):
    if size & (size - 1) == 0:
        return lax.shift_right_arithmetic(place, jnp.int32(size.bit_length() - 1))
    return jnp.where(place < 0, -1, lax.div(place, jnp.int32(size)))


def near_side(index):
    return jnp.where(remainder(index, 2) == 0, index + 1, index - 1)


def far_side(index, count):
    return jnp.where(
        remainder(index, 2) == 0,
        jnp.where(index == 0, count - 1, index - 1),
        jnp.where(index == count - 1, 0, index + 1),
    )


def facing(partner_ref, dims):
    index = lax.axis_index("district")
    near = near_side(index)
    far = far_side(index, dims.districts)
    out = []
    for slot in range(dims.slots):
        for block in range(dims.blocks):
            place = partner_ref[slot, block]
            district = group_of(place, dims.coarse * dims.per_device)
            out.append(
                (
                    (district == near).astype(jnp.int32),
                    (district == far).astype(jnp.int32),
                    place,
                )
            )
    return out


def block_of(ref, slot, block):
    return ref[slot, :, block * LANES : (block + 1) * LANES]


def pack_first_kernel(
    dims, partner_hbm, free_hbm, near_ref, far_ref, free_ref, partner_ref, order, sems
):
    fetch_partner = pltpu.make_async_copy(partner_hbm, partner_ref, sems.at[0])
    fetch_free = [
        pltpu.make_async_copy(free_hbm.at[slot], free_ref.at[slot], sems.at[1 + slot])
        for slot in range(dims.slots)
    ]
    fetch_partner.start()
    for fetch in fetch_free:
        fetch.start()
    fetch_partner.wait()
    near_count = jnp.int32(0)
    far_count = jnp.int32(0)
    for place, (near, far, _) in enumerate(facing(partner_ref, dims)):
        slot = jnp.where(near > 0, near_count, jnp.where(far > 0, SIDE + far_count, 2 * SIDE))
        order[slot] = jnp.int32(place)
        near_count += near
        far_count += far
    for fetch in fetch_free:
        fetch.wait()
    for slot in range(2 * SIDE):
        place = order[slot]
        lane = pl.multiple_of(remainder(place, dims.blocks) * LANES, LANES)
        value = free_ref[quotient(place, dims.blocks), :, pl.ds(lane, LANES)]
        if slot < SIDE:
            near_ref[slot] = value
        else:
            far_ref[slot - SIDE] = value


def prepare_kernel(
    dims,
    partner_hbm,
    iface_hbm,
    owner_hbm,
    modes_hbm,
    inverse_hbm,
    flex_hbm,
    others_in,
    take_ref,
    give_ref,
    weight_ref,
    modes_out,
    high_out,
    low_out,
    flex_out,
    partner_ref,
    iface_ref,
    owner_ref,
    modes_ref,
    inverse_ref,
    others_ref,
    partners,
    sems,
):
    pairs = (
        (partner_hbm, partner_ref),
        (iface_hbm, iface_ref),
        (owner_hbm, owner_ref),
        (others_in, others_ref),
        (modes_hbm, modes_ref),
        (inverse_hbm, inverse_ref),
        (flex_hbm, flex_out),
    )
    fetches = [
        pltpu.make_async_copy(there, here, sems.at[i]) for i, (there, here) in enumerate(pairs)
    ]
    for fetch in fetches:
        fetch.start()
    for fetch in fetches[:-1]:
        fetch.wait()
    faces = facing(partner_ref, dims)
    row = lax.broadcasted_iota(jnp.int32, (TILE, LANES), 0)
    near_count = jnp.int32(0)
    far_count = jnp.int32(0)
    for place, (near, far, whole) in enumerate(faces):
        slot = jnp.where(near > 0, near_count, jnp.where(far > 0, SIDE + far_count, 2 * SIDE))
        partners[slot] = remainder(jnp.maximum(whole, 0), dims.per_device)
        give_ref[place] = jnp.where(row == slot, 1.0, 0.0).astype(F32)
        near_count += near
        far_count += far
    for place, (near, far, whole) in enumerate(faces):
        other = remainder(jnp.maximum(whole, 0), dims.per_device)
        slot_id, block_id = divmod(place, dims.blocks)
        from_near = jnp.int32(0)
        from_far = jnp.int32(SIDE)
        for slot in range(SIDE):
            from_near += (partners[slot] < other).astype(jnp.int32)
            from_far += (partners[SIDE + slot] < other).astype(jnp.int32)
        slot = jnp.where(near > 0, from_near, jnp.where(far > 0, from_far, 2 * SIDE))
        take_ref[place] = jnp.where(row == slot, 1.0, 0.0).astype(F32)
        used = (block_id < iface_ref[slot_id]).astype(F32)
        double = used + jnp.maximum(near, far).astype(F32)
        weight_ref[place] = jnp.where(row == 0, used, double)
    member = lax.axis_index("coarse")
    all_slots = dims.slots * dims.coarse
    corner_rows = all_slots * dims.corners
    slot_of_row = quotient(
        lax.broadcasted_iota(jnp.int32, (corner_rows, dims.width), 0), dims.corners
    )
    placed = []
    for slot in range(dims.slots):
        modes = modes_ref[slot].astype(F32)
        stacked = jnp.concatenate([modes] * all_slots, axis=0)
        block = jnp.where(slot_of_row == member * dims.slots + slot, stacked, 0.0).astype(BF16)
        modes_out[:, slot * dims.width : (slot + 1) * dims.width] = block
        placed.append(block)
    corner = lax.broadcasted_iota(jnp.int32, (dims.corners, dims.coarse_width), 0)
    column = lax.broadcasted_iota(jnp.int32, (dims.corners, dims.coarse_width), 1)
    hot, own_hot = [], []
    for place in range(all_slots):
        who, slot = divmod(place, dims.slots)
        owners = jnp.zeros((dims.corners, dims.coarse_width), jnp.int32)
        for k in range(dims.corners):
            if dims.coarse == 2:
                owner = jnp.where(member == who, owner_ref[slot, k], others_ref[slot, k])
            else:
                owner = others_ref[who, slot, k]
            owners = jnp.where(corner == k, owner, owners)
        hot.append(jnp.where(column == owners, 1.0, 0.0).astype(F32))
        own_hot.append(jnp.where(member == who, hot[-1], 0.0))
    onto = jnp.dot(
        jnp.concatenate(hot, axis=0),
        inverse_ref[0],
        precision=lax.Precision.HIGHEST,
        preferred_element_type=F32,
    )
    between = lax.dot_general(
        onto,
        jnp.concatenate(own_hot, axis=0),
        (((1,), (1,)), ((), ())),
        precision=lax.Precision.HIGHEST,
        preferred_element_type=F32,
    )
    pieces = jnp.concatenate(thirds(between), axis=0)
    for slot in range(dims.slots):
        lanes = slice(slot * dims.width, (slot + 1) * dims.width)
        spread = jnp.dot(pieces, placed[slot], preferred_element_type=F32)
        spread = (
            spread[:corner_rows]
            + spread[corner_rows : 2 * corner_rows]
            + spread[2 * corner_rows :]
        )
        high, low = halves(spread)
        high_out[:, lanes] = high
        low_out[:, lanes] = low
    fetches[-1].wait()


def halves(value):
    high = value.astype(BF16)
    low = (value - high.astype(F32)).astype(BF16)
    return high, low


def thirds(value):
    first = value.astype(BF16)
    rest = value - first.astype(F32)
    second, third = halves(rest)
    return first, second, third


def lane_sums(value):
    return jnp.sum(value, axis=0, keepdims=True)


def row_at(ref, place, row):
    return ref[place, pl.ds(row, 1), :]


def left_rows():
    return jnp.where(remainder(lax.axis_index("district"), 2) == 0, SIDE, 0)


def jump_blocks(dims, field_ref, sides, take_ref, weight_ref):
    for slot in range(dims.slots):
        for block in range(dims.blocks):
            place = slot * dims.blocks + block
            value = block_of(field_ref, slot, block) * weight_ref[place, 0:1, :]
            for first, ref in sides:
                for j in range(SIDE):
                    value = value - row_at(take_ref, place, first + j) * ref[j]
            yield slot, block, value


def corner_sums(dims, parts, modes_ref):
    stacked = jnp.concatenate([jnp.concatenate(part, axis=1) for part in parts], axis=0)
    sums = lax.dot_general(
        stacked, modes_ref[...], (((1,), (1,)), ((), ())), preferred_element_type=F32
    )
    return folded(dims, sums)


def folded(dims, rows):
    groups = [rows[i : i + dims.scen] for i in range(0, rows.shape[0], dims.scen)]
    return functools.reduce(jnp.add, groups)


def jump_kernel(
    dims,
    field_ref,
    near_ref,
    far_ref,
    take_ref,
    weight_ref,
    modes_ref,
    jump_ref,
    corner_ref,
    pieces,
):
    parts = [[] for _ in range(pieces)]
    for slot, block, value in jump_blocks(
        dims, field_ref, ((0, near_ref), (SIDE, far_ref)), take_ref, weight_ref
    ):
        jump_ref[slot, :, block * LANES : (block + 1) * LANES] = value
        for part, piece in zip(parts, halves(value)):
            part.append(piece)
    corner_ref[...] = corner_sums(dims, parts, modes_ref)


def local_term(dims, pieces, direction_ref, flex_ref):
    for slot in range(dims.slots):
        forces = jnp.concatenate(halves(direction_ref[slot])[:pieces], axis=0)
        yield folded(dims, jnp.dot(forces, flex_ref[slot], preferred_element_type=F32))


def corner_weights(dims, field_ref, weight_ref, high_ref, low_ref):
    high_parts, low_parts = [], []
    for slot in range(dims.slots):
        for block in range(dims.blocks):
            place = slot * dims.blocks + block
            value = block_of(field_ref, slot, block) * weight_ref[place, 1:2, :]
            high, low = halves(value)
            high_parts.append(high)
            low_parts.append(low)
    high = jnp.concatenate(high_parts, axis=1)
    both = jnp.concatenate([high, jnp.concatenate(low_parts, axis=1)], axis=0)
    contract = (((1,), (1,)), ((), ()))
    part = lax.dot_general(both, high_ref[...], contract, preferred_element_type=F32)
    rest = lax.dot_general(high, low_ref[...], contract, preferred_element_type=F32)
    return part[: dims.scen] + part[dims.scen :] + rest


def local_kernel(dims, direction_ref, flex_ref, weight_ref, high_ref, low_ref, out_ref, g_ref):
    for slot, term in enumerate(local_term(dims, 1, direction_ref, flex_ref)):
        out_ref[slot] = term
    g_ref[...] = corner_weights(dims, direction_ref, weight_ref, high_ref, low_ref)


def local_last_kernel(
    dims,
    direction_ref,
    flex_ref,
    weight_ref,
    high_ref,
    low_ref,
    rhs_ref,
    out_ref,
    g_ref,
    sums_ref,
):
    acc = [jnp.zeros((dims.scen, LANES), F32)] * 5
    for slot, term in enumerate(local_term(dims, 2, direction_ref, flex_ref)):
        out_ref[slot] = term
        for block in range(dims.blocks):
            rhs = block_of(rhs_ref, slot, block)
            image = block_of(direction_ref, slot, block)
            doubled = (
                weight_ref[slot * dims.blocks + block, 1:2, :]
                * term[:, block * LANES : (block + 1) * LANES]
            )
            for q, product in enumerate(
                (rhs * rhs, rhs * image, image * image, rhs * doubled, image * doubled)
            ):
                acc[q] = acc[q] + product
    sums_ref[...] = totals_of(rows_of(acc, 0))
    g_ref[...] = corner_weights(dims, direction_ref, weight_ref, high_ref, low_ref)


def totals_of(tile):
    totals = jnp.sum(tile, axis=1, keepdims=True)
    return lane_sums(jnp.where(on_diagonal(), totals, 0.0))


def rows_of(parts, first):
    lanes = parts[0].shape[1]
    row = lax.broadcasted_iota(jnp.int32, (TILE, lanes), 0)
    tile = jnp.zeros((TILE, lanes), F32)
    for q, part in enumerate(parts):
        tile = jnp.where(row == first + q, lane_sums(part), tile)
    return tile


def on_diagonal():
    row = lax.broadcasted_iota(jnp.int32, (TILE, LANES), 0)
    return row == lax.broadcasted_iota(jnp.int32, (TILE, LANES), 1)


def add_coarse(dims, local_ref, sums, high_ref, low_ref):
    high, low = halves(sums)
    both = jnp.concatenate([high, low], axis=0)
    for slot in range(dims.slots):
        lanes = slice(slot * dims.width, (slot + 1) * dims.width)
        part = jnp.dot(both, high_ref[:, lanes], preferred_element_type=F32)
        rest = jnp.dot(high, low_ref[:, lanes], preferred_element_type=F32)
        yield local_ref[slot] + (part[: dims.scen] + part[dims.scen :] + rest)


def pack(dims, response, give_ref, sides):
    for first, ref in sides:
        for j in range(SIDE):
            value = jnp.zeros((dims.scen, LANES), F32)
            for place in range(dims.per_device):
                slot, block = divmod(place, dims.blocks)
                part = response[slot][:, block * LANES : (block + 1) * LANES]
                value = value + row_at(give_ref, place, first + j) * part
            ref[j] = value


def respond_kernel(
    dims,
    local_ref,
    own_ref,
    other_ref,
    high_ref,
    low_ref,
    give_ref,
    out_ref,
    near_ref,
    far_ref,
):
    response = list(add_coarse(dims, local_ref, own_ref[...] + other_ref[...], high_ref, low_ref))
    for slot in range(dims.slots):
        out_ref[slot] = response[slot]
    pack(dims, response, give_ref, ((0, near_ref), (SIDE, far_ref)))


def respond_last_kernel(
    dims,
    local_ref,
    own_ref,
    other_ref,
    high_ref,
    low_ref,
    give_ref,
    rhs_g_ref,
    image_g_ref,
    early_ref,
    out_ref,
    right_ref,
    left_ref,
    sums_hbm,
    sums_ref,
    sem,
):
    corner = own_ref[...] + other_ref[...]
    late = totals_of(rows_of((corner * rhs_g_ref[...], corner * image_g_ref[...]), 3))
    sums_ref[...] = jnp.broadcast_to((early_ref[...] + late)[None], sums_ref.shape)
    put = pltpu.make_async_copy(sums_ref, sums_hbm, sem)
    put.start()
    response = list(add_coarse(dims, local_ref, corner, high_ref, low_ref))
    for slot in range(dims.slots):
        out_ref[slot] = response[slot]
    pack(dims, response, give_ref, ((SIDE - left_rows(), right_ref), (left_rows(), left_ref)))
    put.wait()


def settle_kernel(
    dims,
    sums_ref,
    rhs_ref,
    image_ref,
    field_ref,
    right_ref,
    take_ref,
    weight_ref,
    multiplier_ref,
    residual_ref,
    factor_ref,
):
    row = lane_sums(sums_ref[...])
    totals = jnp.sum(jnp.where(on_diagonal(), row, 0.0), axis=1, keepdims=True)
    norm, first, square, cross, second = (totals[q : q + 1, :] for q in range(5))
    step = norm / first
    norm_next = norm - 2.0 * step * first + step * step * square
    grown = 1.0 + norm_next / norm
    curve = grown * grown * first - grown * step * (cross + square) + step * step * second
    step_next = norm_next / curve
    on_first = step + step_next * grown
    on_second = step_next * step
    factor_ref[...] = jnp.broadcast_to(on_second, factor_ref.shape)
    for slot, block, second_image in jump_blocks(
        dims, field_ref, ((SIDE - left_rows(), right_ref),), take_ref, weight_ref
    ):
        lanes = slice(block * LANES, (block + 1) * LANES)
        rhs = rhs_ref[slot, :, lanes]
        image = image_ref[slot, :, lanes]
        multiplier_ref[slot, :, lanes] = on_first * rhs - on_second * image
        residual_ref[slot, :, lanes] = rhs - on_first * image + on_second * second_image


def finish_kernel(
    dims,
    multiplier_ref,
    partial_ref,
    factor_ref,
    left_ref,
    take_ref,
    multiplier_hbm,
    residual_hbm,
    residual_ref,
    sems,
):
    puts = [
        pltpu.make_async_copy(
            multiplier_ref.at[slot], multiplier_hbm.at[slot], sems.at[0, slot]
        )
        for slot in range(dims.slots)
    ]
    for put in puts:
        put.start()
    factor = factor_ref[0:1, :]
    shares = [factor * left_ref[j] for j in range(SIDE)]
    first = left_rows()
    for slot in range(dims.slots):
        for block in range(dims.blocks):
            place = slot * dims.blocks + block
            lanes = slice(block * LANES, (block + 1) * LANES)
            value = partial_ref[slot, :, lanes]
            for j in range(SIDE):
                value = value - row_at(take_ref, place, first + j) * shares[j]
            residual_ref[slot, :, lanes] = value
        put = pltpu.make_async_copy(residual_ref.at[slot], residual_hbm.at[slot], sems.at[1, slot])
        put.start()
        puts.append(put)
    for put in puts:
        put.wait()


class Dims:
    pass


def stay(value):
    return pltpu.with_memory_space_constraint(value, pltpu.MemorySpace.HBM)


def call(kernel, dims, outs, args, in_specs=None, out_specs=None, scratch=(), cost=None):
    return pl.pallas_call(
        functools.partial(kernel, dims),
        out_shape=outs,
        in_specs=in_specs if in_specs is not None else [VMEM] * len(args),
        out_specs=out_specs if out_specs is not None else jax.tree.map(lambda _: VMEM, outs),
        scratch_shapes=list(scratch),
        compiler_params=pltpu.CompilerParams(vmem_limit_bytes=16 << 20),
        cost_estimate=cost,
    )(*args)


def local(
    free_response, flexibility, corner_modes, corner_owner, coarse_inverse, iface_blocks, partner
):
    dims = Dims()
    dims.slots, dims.scen, dims.width = free_response.shape
    dims.blocks = partner.shape[1]
    dims.per_device = dims.slots * dims.blocks
    dims.coarse_width = coarse_inverse.shape[1]
    dims.corners = corner_modes.shape[1]
    dims.districts = lax.axis_size("district")
    dims.coarse = lax.axis_size("coarse")
    devices = dims.districts * dims.coarse
    shape = jax.ShapeDtypeStruct
    whole = shape(free_response.shape, F32)
    packed = shape((SIDE, dims.scen, LANES), F32)
    per_block = shape((dims.per_device, TILE, LANES), F32)
    corner_rows = dims.slots * dims.corners * dims.coarse

    near_pairs = [(d, d + 1 if d % 2 == 0 else d - 1) for d in range(dims.districts)]
    far_pairs = [
        (d, (d - 1 if d % 2 == 0 else d + 1) % dims.districts) for d in range(dims.districts)
    ]

    def passed_along(value, steps):
        count = dims.districts
        return lax.ppermute(value, "district", [(d, (d + steps) % count) for d in range(count)])

    def exchange(near, far):
        far = lax.ppermute(far, "district", far_pairs)
        near = lax.ppermute(near, "district", near_pairs)
        return near, far

    def from_group(value):
        if dims.coarse == 2:
            return lax.ppermute(value, "coarse", [(0, 1), (1, 0)])
        return lax.psum(value, "coarse") - value

    near, far, field = call(
        pack_first_kernel,
        dims,
        (packed, packed, whole),
        (stay(partner), stay(free_response)),
        in_specs=[HBM, HBM],
        scratch=[
            pltpu.SMEM(partner.shape, jnp.int32),
            pltpu.SMEM((2 * SIDE + 1,), jnp.int32),
            pltpu.SemaphoreType.DMA((1 + dims.slots,)),
        ],
    )
    near, far = exchange(near, far)
    if dims.coarse == 2:
        others = lax.ppermute(corner_owner, "coarse", [(0, 1), (1, 0)])
    else:
        others = lax.all_gather(corner_owner, "coarse")
    take, give, weight, modes, high, low, flex = call(
        prepare_kernel,
        dims,
        (
            per_block,
            per_block,
            per_block,
            shape((corner_rows, dims.slots * dims.width), BF16),
            shape((corner_rows, dims.slots * dims.width), BF16),
            shape((corner_rows, dims.slots * dims.width), BF16),
            shape(flexibility.shape, BF16),
        ),
        tuple(
            stay(value)
            for value in (
                partner,
                iface_blocks,
                corner_owner,
                corner_modes,
                coarse_inverse,
                flexibility,
            )
        )
        + (others,),
        in_specs=[HBM] * 6 + [VMEM],
        scratch=[
            pltpu.SMEM(partner.shape, jnp.int32),
            pltpu.SMEM(iface_blocks.shape, jnp.int32),
            pltpu.SMEM(corner_owner.shape, jnp.int32),
            pltpu.VMEM(corner_modes.shape, BF16),
            pltpu.VMEM(coarse_inverse.shape, F32),
            pltpu.SMEM(others.shape, jnp.int32),
            pltpu.SMEM((2 * SIDE + 1,), jnp.int32),
            pltpu.SemaphoreType.DMA((7,)),
        ],
        cost=pl.CostEstimate(flops=10**7, bytes_accessed=4 * 10**6, transcendentals=0),
    )

    def jump(field, near, far, pieces):
        return call(
            functools.partial(jump_kernel, pieces=pieces),
            dims,
            (whole, shape((dims.scen, corner_rows), F32)),
            (field, near, far, take, weight, modes),
        )

    matmul_cost = pl.CostEstimate(flops=10**8, bytes_accessed=3 * 10**6, transcendentals=0)
    rhs, part = jump(field, near, far, 1)
    other = from_group(part)
    corners = shape((dims.scen, corner_rows), F32)
    term, rhs_g = call(
        local_kernel,
        dims,
        (whole, corners),
        (rhs, flex, weight, high, low),
        cost=matmul_cost,
    )
    response, near, far = call(
        respond_kernel,
        dims,
        (whole, packed, packed),
        (term, part, other, high, low, give),
    )
    near, far = exchange(near, far)
    image, part = jump(response, near, far, 2)
    other = from_group(part)
    term, image_g, early = call(
        local_last_kernel,
        dims,
        (whole, corners, shape((1, LANES), F32)),
        (image, flex, weight, high, low, rhs),
        cost=matmul_cost,
    )
    response, right, left, sums = call(
        respond_last_kernel,
        dims,
        (whole, packed, packed, shape((devices, 1, LANES), F32)),
        (term, part, other, high, low, give, rhs_g, image_g, early),
        out_specs=(VMEM, VMEM, VMEM, HBM),
        scratch=[pltpu.VMEM((devices, 1, LANES), F32), pltpu.SemaphoreType.DMA],
    )
    sums = lax.all_to_all(sums, AXES, 0, 0)
    from_left = passed_along(right, 1)
    from_right = passed_along(left, -1)
    multiplier, residual, factor = call(
        settle_kernel,
        dims,
        (whole, whole, shape((TILE, LANES), F32)),
        (sums.reshape(devices, LANES), rhs, image, response, from_right, take, weight),
    )
    return call(
        finish_kernel,
        dims,
        (whole, whole),
        (multiplier, residual, factor, from_left, take),
        out_specs=(HBM, HBM),
        scratch=[pltpu.VMEM(free_response.shape, F32), pltpu.SemaphoreType.DMA((2, dims.slots))],
    )


def solution(mesh):
    in_specs = (
        P(AXES, None, None),
        P(AXES, None, None),
        P(AXES, None, None),
        P(AXES, None),
        P("district", None, None),
        P(AXES),
        P(AXES, None),
    )
    out_specs = (P(AXES, None, None), P(AXES, None, None))
    return jax.shard_map(local, mesh=mesh, in_specs=in_specs, out_specs=out_specs, check_vma=False)
```

```python
import functools

import jax
import jax.numpy as jnp
from jax import lax
from jax.experimental import pallas as pl
from jax.experimental.pallas import tpu as pltpu
from jax.sharding import PartitionSpec as P


SIDE = 4
AXES = ("district", "coarse")
VMEM = pl.BlockSpec(memory_space=pltpu.VMEM)
HBM = pl.BlockSpec(memory_space=pltpu.MemorySpace.HBM)
F32 = jnp.float32
BF16 = jnp.bfloat16
TILE = 8
LANES = 128


def quotient(value, by):
    if by & (by - 1) == 0:
        return lax.shift_right_logical(value, jnp.int32(by.bit_length() - 1))
    return lax.div(value, jnp.int32(by))


def remainder(value, by):
    if by & (by - 1) == 0:
        return lax.bitwise_and(value, jnp.int32(by - 1))
    return lax.rem(value, jnp.int32(by))


def group_of(place, size):
    if size & (size - 1) == 0:
        return lax.shift_right_arithmetic(place, jnp.int32(size.bit_length() - 1))
    return jnp.where(place < 0, -1, lax.div(place, jnp.int32(size)))


def near_side(index):
    return jnp.where(remainder(index, 2) == 0, index + 1, index - 1)


def far_side(index, count):
    return jnp.where(
        remainder(index, 2) == 0,
        jnp.where(index == 0, count - 1, index - 1),
        jnp.where(index == count - 1, 0, index + 1),
    )


def facing(partner_ref, dims):
    index = lax.axis_index("district")
    near = near_side(index)
    far = far_side(index, dims.districts)
    out = []
    for slot in range(dims.slots):
        for block in range(dims.blocks):
            place = partner_ref[slot, block]
            district = group_of(place, dims.coarse * dims.per_device)
            out.append(
                (
                    (district == near).astype(jnp.int32),
                    (district == far).astype(jnp.int32),
                    place,
                )
            )
    return out


def lanes_of(dims, block):
    return slice(block * dims.block_width, (block + 1) * dims.block_width)


def block_of(dims, ref, slot, block):
    return ref[slot, :, lanes_of(dims, block)]


def pack_first_kernel(
    dims, partner_hbm, free_hbm, near_ref, far_ref, free_ref, partner_ref, order, sems
):
    fetch_partner = pltpu.make_async_copy(partner_hbm, partner_ref, sems.at[0])
    fetch_free = [
        pltpu.make_async_copy(free_hbm.at[slot], free_ref.at[slot], sems.at[1 + slot])
        for slot in range(dims.slots)
    ]
    fetch_partner.start()
    for fetch in fetch_free:
        fetch.start()
    fetch_partner.wait()
    near_count = jnp.int32(0)
    far_count = jnp.int32(0)
    for place, (near, far, _) in enumerate(facing(partner_ref, dims)):
        slot = jnp.where(near > 0, near_count, jnp.where(far > 0, SIDE + far_count, 2 * SIDE))
        order[slot] = jnp.int32(place)
        near_count += near
        far_count += far
    for fetch in fetch_free:
        fetch.wait()
    for slot in range(2 * SIDE):
        place = order[slot]
        lane = remainder(place, dims.blocks) * dims.block_width
        lanes = pl.ds(pl.multiple_of(lane, dims.block_width), dims.block_width)
        value = free_ref[quotient(place, dims.blocks), :, lanes]
        if slot < SIDE:
            near_ref[slot] = value
        else:
            far_ref[slot - SIDE] = value


def prepare_kernel(
    dims,
    partner_hbm,
    iface_hbm,
    owner_hbm,
    modes_hbm,
    inverse_hbm,
    flex_hbm,
    others_in,
    take_ref,
    give_ref,
    weight_ref,
    modes_out,
    high_out,
    low_out,
    flex_out,
    partner_ref,
    iface_ref,
    owner_ref,
    modes_ref,
    inverse_ref,
    others_ref,
    partners,
    sems,
):
    pairs = (
        (partner_hbm, partner_ref),
        (iface_hbm, iface_ref),
        (owner_hbm, owner_ref),
        (others_in, others_ref),
        (modes_hbm, modes_ref),
        (inverse_hbm, inverse_ref),
        (flex_hbm, flex_out),
    )
    fetches = [
        pltpu.make_async_copy(there, here, sems.at[i]) for i, (there, here) in enumerate(pairs)
    ]
    for fetch in fetches:
        fetch.start()
    for fetch in fetches[:-1]:
        fetch.wait()
    faces = facing(partner_ref, dims)
    row = lax.broadcasted_iota(jnp.int32, (TILE, dims.block_width), 0)
    near_count = jnp.int32(0)
    far_count = jnp.int32(0)
    for place, (near, far, whole) in enumerate(faces):
        slot = jnp.where(near > 0, near_count, jnp.where(far > 0, SIDE + far_count, 2 * SIDE))
        partners[slot] = remainder(jnp.maximum(whole, 0), dims.per_device)
        give_ref[place] = jnp.where(row == slot, 1.0, 0.0).astype(F32)
        near_count += near
        far_count += far
    for place, (near, far, whole) in enumerate(faces):
        other = remainder(jnp.maximum(whole, 0), dims.per_device)
        slot_id, block_id = divmod(place, dims.blocks)
        from_near = jnp.int32(0)
        from_far = jnp.int32(SIDE)
        for slot in range(SIDE):
            from_near += (partners[slot] < other).astype(jnp.int32)
            from_far += (partners[SIDE + slot] < other).astype(jnp.int32)
        slot = jnp.where(near > 0, from_near, jnp.where(far > 0, from_far, 2 * SIDE))
        take_ref[place] = jnp.where(row == slot, 1.0, 0.0).astype(F32)
        used = (block_id < iface_ref[slot_id]).astype(F32)
        double = used + jnp.maximum(near, far).astype(F32)
        weight_ref[place] = jnp.where(row == 0, used, double)
    member = lax.axis_index("coarse")
    all_slots = dims.slots * dims.coarse
    corner_rows = all_slots * dims.corners
    slot_of_row = quotient(
        lax.broadcasted_iota(jnp.int32, (corner_rows, dims.width), 0), dims.corners
    )
    placed = []
    for slot in range(dims.slots):
        modes = modes_ref[slot].astype(F32)
        stacked = jnp.concatenate([modes] * all_slots, axis=0)
        block = jnp.where(slot_of_row == member * dims.slots + slot, stacked, 0.0).astype(BF16)
        modes_out[:, slot * dims.width : (slot + 1) * dims.width] = block
        placed.append(block)
    corner = lax.broadcasted_iota(jnp.int32, (dims.corners, dims.coarse_width), 0)
    column = lax.broadcasted_iota(jnp.int32, (dims.corners, dims.coarse_width), 1)
    hot, own_hot = [], []
    for place in range(all_slots):
        who, slot = divmod(place, dims.slots)
        owners = jnp.zeros((dims.corners, dims.coarse_width), jnp.int32)
        for k in range(dims.corners):
            if dims.coarse == 2:
                owner = jnp.where(member == who, owner_ref[slot, k], others_ref[slot, k])
            else:
                owner = others_ref[who, slot, k]
            owners = jnp.where(corner == k, owner, owners)
        hot.append(jnp.where(column == owners, 1.0, 0.0).astype(F32))
        own_hot.append(jnp.where(member == who, hot[-1], 0.0))
    onto = jnp.dot(
        jnp.concatenate(hot, axis=0),
        inverse_ref[0],
        precision=lax.Precision.HIGHEST,
        preferred_element_type=F32,
    )
    between = lax.dot_general(
        onto,
        jnp.concatenate(own_hot, axis=0),
        (((1,), (1,)), ((), ())),
        precision=lax.Precision.HIGHEST,
        preferred_element_type=F32,
    )
    pieces = jnp.concatenate(thirds(between), axis=0)
    for slot in range(dims.slots):
        lanes = slice(slot * dims.width, (slot + 1) * dims.width)
        spread = jnp.dot(pieces, placed[slot], preferred_element_type=F32)
        spread = (
            spread[:corner_rows]
            + spread[corner_rows : 2 * corner_rows]
            + spread[2 * corner_rows :]
        )
        high, low = halves(spread)
        high_out[:, lanes] = high
        low_out[:, lanes] = low
    fetches[-1].wait()


def halves(value):
    high = value.astype(BF16)
    low = (value - high.astype(F32)).astype(BF16)
    return high, low


def thirds(value):
    first = value.astype(BF16)
    rest = value - first.astype(F32)
    second, third = halves(rest)
    return first, second, third


def lane_sums(value):
    return jnp.sum(value, axis=0, keepdims=True)


def row_at(ref, place, row):
    return ref[place, pl.ds(row, 1), :]


def left_rows():
    return jnp.where(remainder(lax.axis_index("district"), 2) == 0, SIDE, 0)


def jump_blocks(dims, field_ref, sides, take_ref, weight_ref):
    for slot in range(dims.slots):
        for block in range(dims.blocks):
            place = slot * dims.blocks + block
            value = block_of(dims, field_ref, slot, block) * weight_ref[place, 0:1, :]
            for first, ref in sides:
                for j in range(SIDE):
                    value = value - row_at(take_ref, place, first + j) * ref[j]
            yield slot, block, value


def corner_sums(dims, parts, modes_ref):
    stacked = jnp.concatenate([jnp.concatenate(part, axis=1) for part in parts], axis=0)
    sums = lax.dot_general(
        stacked, modes_ref[...], (((1,), (1,)), ((), ())), preferred_element_type=F32
    )
    return folded(dims, sums)


def folded(dims, rows):
    groups = [rows[i : i + dims.scen] for i in range(0, rows.shape[0], dims.scen)]
    return functools.reduce(jnp.add, groups)


def jump_kernel(
    dims,
    field_ref,
    near_ref,
    far_ref,
    take_ref,
    weight_ref,
    modes_ref,
    jump_ref,
    corner_ref,
    pieces,
):
    parts = [[] for _ in range(pieces)]
    for slot, block, value in jump_blocks(
        dims, field_ref, ((0, near_ref), (SIDE, far_ref)), take_ref, weight_ref
    ):
        jump_ref[slot, :, lanes_of(dims, block)] = value
        for part, piece in zip(parts, halves(value)):
            part.append(piece)
    corner_ref[...] = corner_sums(dims, parts, modes_ref)


def local_term(dims, pieces, direction_ref, flex_ref):
    for slot in range(dims.slots):
        forces = jnp.concatenate(halves(direction_ref[slot])[:pieces], axis=0)
        yield folded(dims, jnp.dot(forces, flex_ref[slot], preferred_element_type=F32))


def corner_weights(dims, field_ref, weight_ref, high_ref, low_ref):
    high_parts, low_parts = [], []
    for slot in range(dims.slots):
        for block in range(dims.blocks):
            place = slot * dims.blocks + block
            value = block_of(dims, field_ref, slot, block) * weight_ref[place, 1:2, :]
            high, low = halves(value)
            high_parts.append(high)
            low_parts.append(low)
    high = jnp.concatenate(high_parts, axis=1)
    both = jnp.concatenate([high, jnp.concatenate(low_parts, axis=1)], axis=0)
    contract = (((1,), (1,)), ((), ()))
    part = lax.dot_general(both, high_ref[...], contract, preferred_element_type=F32)
    rest = lax.dot_general(high, low_ref[...], contract, preferred_element_type=F32)
    return part[: dims.scen] + part[dims.scen :] + rest


def local_kernel(dims, direction_ref, flex_ref, weight_ref, high_ref, low_ref, out_ref, g_ref):
    for slot, term in enumerate(local_term(dims, 1, direction_ref, flex_ref)):
        out_ref[slot] = term
    g_ref[...] = corner_weights(dims, direction_ref, weight_ref, high_ref, low_ref)


def local_last_kernel(
    dims,
    direction_ref,
    flex_ref,
    weight_ref,
    high_ref,
    low_ref,
    rhs_ref,
    out_ref,
    g_ref,
    sums_ref,
):
    acc = [jnp.zeros((dims.scen, dims.block_width), F32)] * 5
    for slot, term in enumerate(local_term(dims, 2, direction_ref, flex_ref)):
        out_ref[slot] = term
        for block in range(dims.blocks):
            rhs = block_of(dims, rhs_ref, slot, block)
            image = block_of(dims, direction_ref, slot, block)
            doubled = (
                weight_ref[slot * dims.blocks + block, 1:2, :]
                * term[:, lanes_of(dims, block)]
            )
            for q, product in enumerate(
                (rhs * rhs, rhs * image, image * image, rhs * doubled, image * doubled)
            ):
                acc[q] = acc[q] + product
    sums_ref[...] = totals_of(rows_of(acc, 0))
    g_ref[...] = corner_weights(dims, direction_ref, weight_ref, high_ref, low_ref)


def totals_of(tile):
    totals = jnp.sum(tile, axis=1, keepdims=True)
    return lane_sums(jnp.where(on_diagonal(), totals, 0.0))


def rows_of(parts, first):
    lanes = parts[0].shape[1]
    row = lax.broadcasted_iota(jnp.int32, (TILE, lanes), 0)
    tile = jnp.zeros((TILE, lanes), F32)
    for q, part in enumerate(parts):
        tile = jnp.where(row == first + q, lane_sums(part), tile)
    return tile


def on_diagonal():
    row = lax.broadcasted_iota(jnp.int32, (TILE, LANES), 0)
    return row == lax.broadcasted_iota(jnp.int32, (TILE, LANES), 1)


def add_coarse(dims, local_ref, sums, high_ref, low_ref):
    high, low = halves(sums)
    both = jnp.concatenate([high, low], axis=0)
    for slot in range(dims.slots):
        lanes = slice(slot * dims.width, (slot + 1) * dims.width)
        part = jnp.dot(both, high_ref[:, lanes], preferred_element_type=F32)
        rest = jnp.dot(high, low_ref[:, lanes], preferred_element_type=F32)
        yield local_ref[slot] + (part[: dims.scen] + part[dims.scen :] + rest)


def pack(dims, response, give_ref, sides):
    for first, ref in sides:
        for j in range(SIDE):
            value = jnp.zeros((dims.scen, dims.block_width), F32)
            for place in range(dims.per_device):
                slot, block = divmod(place, dims.blocks)
                part = response[slot][:, lanes_of(dims, block)]
                value = value + row_at(give_ref, place, first + j) * part
            ref[j] = value


def respond_kernel(
    dims,
    local_ref,
    own_ref,
    other_ref,
    high_ref,
    low_ref,
    give_ref,
    out_ref,
    near_ref,
    far_ref,
):
    response = list(add_coarse(dims, local_ref, own_ref[...] + other_ref[...], high_ref, low_ref))
    for slot in range(dims.slots):
        out_ref[slot] = response[slot]
    pack(dims, response, give_ref, ((0, near_ref), (SIDE, far_ref)))


def respond_last_kernel(
    dims,
    local_ref,
    own_ref,
    other_ref,
    high_ref,
    low_ref,
    give_ref,
    rhs_g_ref,
    image_g_ref,
    early_ref,
    out_ref,
    right_ref,
    left_ref,
    sums_hbm,
    sums_ref,
    sem,
):
    corner = own_ref[...] + other_ref[...]
    late = totals_of(rows_of((corner * rhs_g_ref[...], corner * image_g_ref[...]), 3))
    sums_ref[...] = jnp.broadcast_to((early_ref[...] + late)[None], sums_ref.shape)
    put = pltpu.make_async_copy(sums_ref, sums_hbm, sem)
    put.start()

    @pl.when(lax.axis_index("district") >= 0)
    def _():
        sums = own_ref[...] + other_ref[...]
        response = list(add_coarse(dims, local_ref, sums, high_ref, low_ref))
        for slot in range(dims.slots):
            out_ref[slot] = response[slot]
        sides = ((SIDE - left_rows(), right_ref), (left_rows(), left_ref))
        pack(dims, response, give_ref, sides)

    put.wait()


def settle_kernel(
    dims,
    sums_ref,
    rhs_ref,
    image_ref,
    field_ref,
    right_ref,
    take_ref,
    weight_ref,
    multiplier_ref,
    residual_ref,
    factor_ref,
):
    row = lane_sums(sums_ref[...])
    totals = jnp.sum(jnp.where(on_diagonal(), row, 0.0), axis=1, keepdims=True)
    norm, first, square, cross, second = (totals[q : q + 1, :] for q in range(5))
    step = norm / first
    norm_next = norm - 2.0 * step * first + step * step * square
    grown = 1.0 + norm_next / norm
    curve = grown * grown * first - grown * step * (cross + square) + step * step * second
    step_next = norm_next / curve
    on_first = step + step_next * grown
    on_second = step_next * step
    factor_ref[...] = jnp.broadcast_to(on_second, factor_ref.shape)
    for slot, block, second_image in jump_blocks(
        dims, field_ref, ((SIDE - left_rows(), right_ref),), take_ref, weight_ref
    ):
        lanes = lanes_of(dims, block)
        rhs = rhs_ref[slot, :, lanes]
        image = image_ref[slot, :, lanes]
        multiplier_ref[slot, :, lanes] = on_first * rhs - on_second * image
        residual_ref[slot, :, lanes] = rhs - on_first * image + on_second * second_image


def finish_kernel(
    dims,
    multiplier_ref,
    partial_ref,
    factor_ref,
    left_ref,
    take_ref,
    multiplier_hbm,
    residual_hbm,
    residual_ref,
    sems,
):
    puts = [
        pltpu.make_async_copy(
            multiplier_ref.at[slot], multiplier_hbm.at[slot], sems.at[0, slot]
        )
        for slot in range(dims.slots)
    ]
    for put in puts:
        put.start()
    factor = factor_ref[0:1, :]
    shares = [factor * left_ref[j] for j in range(SIDE)]
    first = left_rows()
    for slot in range(dims.slots):
        for block in range(dims.blocks):
            place = slot * dims.blocks + block
            lanes = lanes_of(dims, block)
            value = partial_ref[slot, :, lanes]
            for j in range(SIDE):
                value = value - row_at(take_ref, place, first + j) * shares[j]
            residual_ref[slot, :, lanes] = value
        put = pltpu.make_async_copy(residual_ref.at[slot], residual_hbm.at[slot], sems.at[1, slot])
        put.start()
        puts.append(put)
    for put in puts:
        put.wait()


class Dims:
    pass


def stay(value):
    return pltpu.with_memory_space_constraint(value, pltpu.MemorySpace.HBM)


def call(kernel, dims, outs, args, in_specs=None, out_specs=None, scratch=(), cost=None):
    return pl.pallas_call(
        functools.partial(kernel, dims),
        out_shape=outs,
        in_specs=in_specs if in_specs is not None else [VMEM] * len(args),
        out_specs=out_specs if out_specs is not None else jax.tree.map(lambda _: VMEM, outs),
        scratch_shapes=list(scratch),
        compiler_params=pltpu.CompilerParams(vmem_limit_bytes=16 << 20),
        cost_estimate=cost,
    )(*args)


def local(
    free_response, flexibility, corner_modes, corner_owner, coarse_inverse, iface_blocks, partner
):
    dims = Dims()
    dims.slots, dims.scen, dims.width = free_response.shape
    dims.blocks = partner.shape[1]
    dims.block_width = dims.width // dims.blocks
    dims.per_device = dims.slots * dims.blocks
    dims.coarse_width = coarse_inverse.shape[1]
    dims.corners = corner_modes.shape[1]
    dims.districts = lax.axis_size("district")
    dims.coarse = lax.axis_size("coarse")
    devices = dims.districts * dims.coarse
    shape = jax.ShapeDtypeStruct
    whole = shape(free_response.shape, F32)
    packed = shape((SIDE, dims.scen, dims.block_width), F32)
    per_block = shape((dims.per_device, TILE, dims.block_width), F32)
    corner_rows = dims.slots * dims.corners * dims.coarse

    near_pairs = [(d, d + 1 if d % 2 == 0 else d - 1) for d in range(dims.districts)]
    far_pairs = [
        (d, (d - 1 if d % 2 == 0 else d + 1) % dims.districts) for d in range(dims.districts)
    ]

    def passed_along(value, steps):
        count = dims.districts
        return lax.ppermute(value, "district", [(d, (d + steps) % count) for d in range(count)])

    def exchange(near, far):
        far = lax.ppermute(far, "district", far_pairs)
        near = lax.ppermute(near, "district", near_pairs)
        return near, far

    def from_group(value):
        if dims.coarse == 2:
            return lax.ppermute(value, "coarse", [(0, 1), (1, 0)])
        return lax.psum(value, "coarse") - value

    near, far, field = call(
        pack_first_kernel,
        dims,
        (packed, packed, whole),
        (stay(partner), stay(free_response)),
        in_specs=[HBM, HBM],
        scratch=[
            pltpu.SMEM(partner.shape, jnp.int32),
            pltpu.SMEM((2 * SIDE + 1,), jnp.int32),
            pltpu.SemaphoreType.DMA((1 + dims.slots,)),
        ],
    )
    near, far = exchange(near, far)
    if dims.coarse == 2:
        others = lax.ppermute(corner_owner, "coarse", [(0, 1), (1, 0)])
    else:
        others = lax.all_gather(corner_owner, "coarse")
    take, give, weight, modes, high, low, flex = call(
        prepare_kernel,
        dims,
        (
            per_block,
            per_block,
            per_block,
            shape((corner_rows, dims.slots * dims.width), BF16),
            shape((corner_rows, dims.slots * dims.width), BF16),
            shape((corner_rows, dims.slots * dims.width), BF16),
            shape(flexibility.shape, BF16),
        ),
        tuple(
            stay(value)
            for value in (
                partner,
                iface_blocks,
                corner_owner,
                corner_modes,
                coarse_inverse,
                flexibility,
            )
        )
        + (others,),
        in_specs=[HBM] * 6 + [VMEM],
        scratch=[
            pltpu.SMEM(partner.shape, jnp.int32),
            pltpu.SMEM(iface_blocks.shape, jnp.int32),
            pltpu.SMEM(corner_owner.shape, jnp.int32),
            pltpu.VMEM(corner_modes.shape, BF16),
            pltpu.VMEM(coarse_inverse.shape, F32),
            pltpu.SMEM(others.shape, jnp.int32),
            pltpu.SMEM((2 * SIDE + 1,), jnp.int32),
            pltpu.SemaphoreType.DMA((7,)),
        ],
        cost=pl.CostEstimate(flops=10**7, bytes_accessed=4 * 10**6, transcendentals=0),
    )

    def jump(field, near, far, pieces):
        return call(
            functools.partial(jump_kernel, pieces=pieces),
            dims,
            (whole, shape((dims.scen, corner_rows), F32)),
            (field, near, far, take, weight, modes),
        )

    matmul_cost = pl.CostEstimate(flops=10**8, bytes_accessed=3 * 10**6, transcendentals=0)
    rhs, part = jump(field, near, far, 1)
    other = from_group(part)
    corners = shape((dims.scen, corner_rows), F32)
    term, rhs_g = call(
        local_kernel,
        dims,
        (whole, corners),
        (rhs, flex, weight, high, low),
        cost=matmul_cost,
    )
    response, near, far = call(
        respond_kernel,
        dims,
        (whole, packed, packed),
        (term, part, other, high, low, give),
    )
    near, far = exchange(near, far)
    image, part = jump(response, near, far, 2)
    other = from_group(part)
    term, image_g, early = call(
        local_last_kernel,
        dims,
        (whole, corners, shape((1, LANES), F32)),
        (image, flex, weight, high, low, rhs),
        cost=matmul_cost,
    )
    response, right, left, sums = call(
        respond_last_kernel,
        dims,
        (whole, packed, packed, shape((devices, 1, LANES), F32)),
        (term, part, other, high, low, give, rhs_g, image_g, early),
        out_specs=(VMEM, VMEM, VMEM, HBM),
        scratch=[pltpu.VMEM((devices, 1, LANES), F32), pltpu.SemaphoreType.DMA],
    )
    sums = lax.all_to_all(sums, AXES, 0, 0)
    from_left = passed_along(right, 1)
    from_right = passed_along(left, -1)
    multiplier, residual, factor = call(
        settle_kernel,
        dims,
        (whole, whole, shape((TILE, dims.block_width), F32)),
        (sums.reshape(devices, LANES), rhs, image, response, from_right, take, weight),
    )
    return call(
        finish_kernel,
        dims,
        (whole, whole),
        (multiplier, residual, factor, from_left, take),
        out_specs=(HBM, HBM),
        scratch=[pltpu.VMEM(free_response.shape, F32), pltpu.SemaphoreType.DMA((2, dims.slots))],
    )


def solution(mesh):
    in_specs = (
        P(AXES, None, None),
        P(AXES, None, None),
        P(AXES, None, None),
        P(AXES, None),
        P("district", None, None),
        P(AXES),
        P(AXES, None),
    )
    out_specs = (P(AXES, None, None), P(AXES, None, None))
    return jax.shard_map(local, mesh=mesh, in_specs=in_specs, out_specs=out_specs, check_vma=False)
```
